32 devices in a mesh: wide: 8 (over z, x), narrow: 4 (over y, core).
Axes of the slice: x: 2, y: 2, z: 4, core: 2. Of those that a mesh axis runs over, the one named last changes fastest.
Arguments:
- embeddings: bfloat16 [8192, 512], P(('wide', 'narrow')), may hold values from -26 to 26
- partners: int32 [32, 7], P(('wide', 'narrow')), may hold values from -1 to 7, as said below
- pair_kind: int32 [32, 7], P(('wide', 'narrow')), may hold values from 0 to 1, as said below
- neighbors: int32 [7, 15, 8192], P(None, None, ('wide', 'narrow')), may hold values from 0 to 255
Outputs:
- gradient: float32 [8192, 512], P(('wide', 'narrow'))
- mean_loss: float32 [], replicated
The draws below stay inside these ranges and needn't reach their ends.
Inputs may be any that keep to these rules, and one draw needn't show every extreme that they name: Row w * 4 + n lists the wide indices of that block's partners in ascending order, then -1 in the remaining slots; a partner has the same narrow index n, is never the block itself, appears once, and the pairing is mutual. In every narrow index one block is paired with all 7 others. `pair_kind`: 1 marks a graph pair, 0 a sampled negative or an empty slot; both directions of a pair carry the same mark, and every block has at least one graph pair.
All inputs are finite; a program needn't handle non-finite values.
Results may differ from the reference program's by a relative error of at most 0.0004.
Values may be sent and summed in bfloat16 or wider, within the bound.
No kernel may reach another device: no remote copies, remote signals or barrier semaphores. Data moves between devices by JAX's collectives and lax.ppermute only.
A program may use at most 64 MiB of HBM per device.

```python
import math
import jax
import jax.numpy as jnp
from jax import lax

D = 512
BLOCK = 256
KNN = 15
SLOTS = 7
NBLK = 32
CELLS = 8192
N_WIDE = 8
N_NARROW = 4


def column_graph(key):
    members = N_WIDE
    cycle_size = members - 1
    shuffled = jax.random.permutation(key, members).astype(jnp.int32)
    position = jnp.zeros((members,), jnp.int32).at[shuffled].set(jnp.arange(members, dtype=jnp.int32))
    row_place = position[:, None]
    col_place = position[None, :]
    distinct = row_place != col_place
    central = (row_place == 0) | (col_place == 0)
    spacing = (row_place - col_place) % cycle_size
    adjacent = ((spacing == 1) | (spacing == cycle_size - 1)) & jnp.logical_not(central)
    skipping = ((spacing == 2) | (spacing == cycle_size - 2)) & jnp.logical_not(central)
    anchor = central & ((row_place == 1) | (col_place == 1))
    linked = distinct & (central | adjacent | skipping)
    coin_flips = jax.random.randint(jax.random.fold_in(key, 11), (members, members), 0, 2)
    upper_half = lax.broadcasted_iota(jnp.int32, (members, members), 0) < lax.broadcasted_iota(jnp.int32, (members, members), 1)
    mutual = jnp.where(upper_half, coin_flips, coin_flips.T)
    marked = jnp.where(adjacent | anchor, 1, mutual) * linked.astype(jnp.int32)
    column_index = lax.broadcasted_iota(jnp.int32, (members, members), 1)
    scores = jnp.where(linked, column_index, members + column_index)
    ordering = jnp.argsort(scores, axis=1, stable=True)[:, :cycle_size].astype(jnp.int32)
    present = jnp.take_along_axis(linked, ordering, axis=1)
    listing = jnp.where(present, ordering, -1)
    pair_marks = jnp.where(present, jnp.take_along_axis(marked, ordering, axis=1), 0)
    return (listing, pair_marks)


def all_columns(key):
    column_keys = jax.random.split(jax.random.fold_in(key, 5), N_NARROW)
    listing, pair_marks = jax.vmap(column_graph)(column_keys)
    listing = jnp.transpose(listing, (1, 0, 2)).reshape(NBLK, SLOTS)
    pair_marks = jnp.transpose(pair_marks, (1, 0, 2)).reshape(NBLK, SLOTS)
    return (listing.astype(jnp.int32), pair_marks.astype(jnp.int32))


def draw_partners(key, part):
    return all_columns(key)[0]


def draw_pair_kind(key, part):
    return all_columns(key)[1]


def draw_embeddings(key, part):
    column_scale = jax.random.uniform(jax.random.fold_in(key, 2), (1, D), jnp.float32, math.log(0.6), math.log(1.6))
    row_scale = jax.random.uniform(jax.random.fold_in(key, 1), (CELLS, 1), jnp.float32, math.log(0.4), math.log(4.0))
    base = jax.random.truncated_normal(jax.random.fold_in(key, 3), -4.0, 4.0, (CELLS, D), jnp.float32)
    return (base * jnp.exp(row_scale) * jnp.exp(column_scale)).astype(jnp.bfloat16)


def with_ends(result, own_key, low, high):
    spot = [jax.random.randint(jax.random.fold_in(own_key, axis), (), 0, length) for axis, length in enumerate(result.shape)]
    widest = result.shape.index(max(result.shape))
    neighbour = spot[:widest] + [(spot[widest] + 1) % result.shape[widest]] + spot[widest + 1:]
    return result.at[tuple(spot)].set(low).at[tuple(neighbour)].set(high)


def setup_inputs(seed: int = 0) -> dict:
    seeds = jax.random.split(jax.random.key(seed), 5)
    embeddings = draw_embeddings(jax.random.fold_in(seeds[4], 71), 0)
    partners = draw_partners(jax.random.fold_in(seeds[4], 71), 0)
    pair_kind = draw_pair_kind(jax.random.fold_in(seeds[4], 71), 0)
    neighbors = with_ends(jax.random.randint(seeds[3], (SLOTS, KNN, CELLS), 0, BLOCK), jax.random.fold_in(seeds[3], 1), 0, BLOCK - 1).astype(jnp.int32)
    return {"embeddings": embeddings, "partners": partners, "pair_kind": pair_kind, "neighbors": neighbors}


def tile_kernel(local_rows, remote_rows, local_norms, remote_norms):
    inner = jnp.dot(local_rows, remote_rows.T, preferred_element_type=jnp.float32)
    distance = local_norms[:, None] + remote_norms[None, :] - 2.0 * inner
    return 1.0 / (1.0 + distance / D)


def edge_counts(targets):
    columns = jnp.arange(BLOCK, dtype=jnp.int32)
    return jnp.sum((targets[:, :, None] == columns[None, None, :]).astype(jnp.float32), axis=0)


def reference(embeddings, partners, pair_kind, neighbors):
    blocks = embeddings.reshape(NBLK, BLOCK, D)
    norms = jnp.sum(jnp.square(blocks.astype(jnp.float32)), axis=2)
    stacked = neighbors.reshape(SLOTS, KNN, NBLK, BLOCK)
    flat_indices = jnp.arange(NBLK * SLOTS, dtype=jnp.int32)

    def locate(flat_index):
        source = flat_index // SLOTS
        slot = flat_index % SLOTS
        partner = partners[source, slot]
        target = jnp.maximum(partner, 0) * N_NARROW + source % N_NARROW
        kernel = tile_kernel(blocks[source], blocks[target], norms[source], norms[target])
        counts = edge_counts(stacked[slot, :, source, :]) * pair_kind[source, slot].astype(jnp.float32)
        return source, target, kernel, counts

    def active_slot(flat_index):
        return partners[flat_index // SLOTS, flat_index % SLOTS] >= 0

    def first(carry, flat_index):
        def active(carry):
            source, target, kernel, counts = locate(flat_index)
            return (carry[0] + jnp.sum(kernel), carry[1] + jnp.sum(counts * jnp.log(kernel)),
                    carry[2] + jnp.sum(counts), carry[3] + BLOCK * BLOCK * 1.0)
        return lax.cond(active_slot(flat_index), active, lambda carry: carry, carry), None

    nothing = jnp.zeros((), jnp.float32)
    sums, _ = lax.scan(first, (nothing, nothing, nothing, nothing), flat_indices)
    total, attract, edges_total, entries = sums
    mean_loss = -attract / edges_total + jnp.log(total / entries)
    repulsion = edges_total / total

    def second(gradient, flat_index):
        def active(gradient):
            source, target, kernel, counts = locate(flat_index)
            weight = (counts * kernel - repulsion * kernel * kernel) / D
            rounded = weight.astype(jnp.bfloat16)
            local_rows = blocks[source]
            remote_rows = blocks[target]
            pulled = 2.0 * (jnp.sum(weight, axis=1)[:, None] * local_rows.astype(jnp.float32)
                            - jnp.dot(rounded, remote_rows, preferred_element_type=jnp.float32))
            pushed = 2.0 * (jnp.sum(weight, axis=0)[:, None] * remote_rows.astype(jnp.float32)
                            - jnp.dot(rounded.T, local_rows, preferred_element_type=jnp.float32))
            return gradient.at[source].add(pulled).at[target].add(pushed)
        return lax.cond(active_slot(flat_index), active, lambda gradient: gradient, gradient), None

    gradient, _ = lax.scan(second, jnp.zeros((NBLK, BLOCK, D), jnp.float32), flat_indices)
    return gradient.reshape(CELLS, D), mean_loss
```

```python
import functools

import jax
import jax.numpy as jnp
from jax import lax
from jax.experimental import pallas as pl
from jax.experimental.pallas import tpu as pltpu
from jax.sharding import PartitionSpec as P


AXES = ("wide", "narrow")
VMEM = pl.BlockSpec(memory_space=pltpu.VMEM)
SMEM = pl.BlockSpec(memory_space=pltpu.SMEM)


def ring_position(index, groups):
    return jnp.where(index % 2 == 0, index // 2, groups - 1 - index // 2)


def ring_index(position, groups):
    return jnp.where(position < groups // 2, 2 * position, 2 * (groups - position) - 1)


def ring_order(groups):
    half = groups // 2
    return [2 * q if q < half else 2 * (groups - q) - 1 for q in range(groups)]


def shift_pairs(groups, offset):
    order = ring_order(groups)
    return [(order[q], order[(q + offset) % groups]) for q in range(groups)]


def ring_offsets(groups):
    half = groups // 2
    offsets = []
    for step in range(1, half):
        offsets += [step, -step]
    return offsets + [half]


def params(mib):
    return pltpu.CompilerParams(vmem_limit_bytes=mib << 20)


def prepare_body(groups, offsets, partners, marks, neighbors, *outs):
    lists, facts = outs[:-1], outs[-1]
    knn, block_rows = neighbors.shape[1:]
    me = ring_position(lax.axis_index("wide"), groups)
    slots = partners.shape[1]
    marked_total = jnp.int32(0)
    present_total = jnp.int32(0)
    for place, offset in enumerate(offsets):
        target = ring_index(lax.rem(me + offset + groups, groups), groups)
        slot = jnp.int32(0)
        present = jnp.int32(0)
        marked = jnp.int32(0)
        for s in range(slots):
            hit = (partners[0, s] == target).astype(jnp.int32)
            slot += hit * s
            present += hit
            marked += hit * marks[0, s]
        marked_total += marked
        present_total += present
        facts[0, place] = present
        rows = jnp.where(marked > 0, neighbors[slot], block_rows).astype(jnp.float32)
        lists[place][...] = jnp.full(lists[place].shape, block_rows, lists[place].dtype)
        lists[place][0:knn, :] = rows.astype(lists[place].dtype)
    facts[0, len(offsets)] = present_total
    facts[0, len(offsets) + 1] = marked_total


def counts_body(places, knn, *refs):
    own, incoming, out = refs[:places], refs[places : 2 * places], refs[2 * places]
    block_rows = out.shape[1]
    chunk = 32

    def histogram(rows, start):
        index = lax.broadcasted_iota(jnp.int32, (chunk, block_rows), 0) + start
        index = index.astype(jnp.float32)
        total = jnp.zeros((chunk, block_rows), jnp.float32)
        for k in range(knn):
            total += jnp.where(rows[k : k + 1, :] == index, 1.0, 0.0)
        return total

    for place in range(places):
        mine = own[place][...].astype(jnp.float32)
        theirs = incoming[place][...].astype(jnp.float32)
        forward = jnp.concatenate(
            [histogram(mine, start) for start in range(0, block_rows, chunk)], axis=0
        )
        back = jnp.concatenate(
            [histogram(theirs, start) for start in range(0, block_rows, chunk)], axis=0
        )
        out[place] = (forward.T + back).astype(out.dtype)


def tile_terms(local, remote, counts, present, features):
    local_float = local.astype(jnp.float32)
    local_norms = jnp.sum(local_float * local_float, axis=1, keepdims=True)
    remote_float = remote.astype(jnp.float32)
    squares = remote_float * remote_float
    high = squares.astype(jnp.bfloat16)
    low = (squares - high.astype(jnp.float32)).astype(jnp.bfloat16)
    ones = jnp.ones((8, local.shape[1]), jnp.bfloat16)
    contract = (((1,), (1,)), ((), ()))
    remote_norms = lax.dot_general(
        ones, high, contract, preferred_element_type=jnp.float32
    ) + lax.dot_general(ones, low, contract, preferred_element_type=jnp.float32)
    inner = lax.dot_general(local, remote, contract, preferred_element_type=jnp.float32)
    distance = local_norms + remote_norms[0:1, :] - 2.0 * inner
    ratio = 1.0 + distance / features
    kernel = present / ratio
    return kernel, counts * jnp.log(ratio), counts * kernel, kernel * kernel


def split(weight):
    high = weight.astype(jnp.bfloat16)
    return high, (weight - high.astype(jnp.float32)).astype(jnp.bfloat16)


def step_body(places, features, first, *refs):
    count = len(places)
    facts, local_ref, counts_ref = refs[:3]
    remotes = refs[3 : 3 + count]
    refs = refs[3 + count :]
    if not first:
        pulls_in, rows_in, sums_in = refs[:3]
        refs = refs[3:]
    pulls, row_sums, sums = refs
    local = local_ref[...]
    block_rows = local.shape[0]
    if first:
        pulls[...] = jnp.zeros_like(pulls)
        row_sums[...] = jnp.zeros_like(row_sums)
        sums[...] = jnp.zeros_like(sums)
    else:
        pulls[...] = pulls_in[...]
        row_sums[...] = rows_in[...]
        sums[...] = sums_in[...]
    for place, remote_ref in zip(places, remotes):
        remote = remote_ref[...]
        present = facts[0, place].astype(jnp.float32)
        counts = counts_ref[place].astype(jnp.float32)
        kernel, attract, near, far = tile_terms(local, remote, counts, present, features)
        stacked = jnp.concatenate(list(split(near)) + list(split(far)), axis=0)
        product = jnp.dot(stacked, remote, preferred_element_type=jnp.float32)
        pulls[0] += product[:block_rows] + product[block_rows : 2 * block_rows]
        pulls[1] += product[2 * block_rows : 3 * block_rows] + product[3 * block_rows :]
        row_sums[0] += jnp.sum(near, axis=1, keepdims=True)
        row_sums[1] += jnp.sum(far, axis=1, keepdims=True)
        sums[0] += jnp.sum(kernel, axis=0, keepdims=True)
        sums[1] += jnp.sum(attract, axis=0, keepdims=True)


def totals_body(places, knn, block_rows, facts, sums, out):
    lane = lax.broadcasted_iota(jnp.int32, out.shape, 1)
    total = jnp.sum(sums[0])
    attract = jnp.sum(sums[1]) * -0.5
    edges = facts[0, places + 1].astype(jnp.float32) * float(knn * block_rows)
    entries = facts[0, places].astype(jnp.float32) * float(block_rows * block_rows)
    values = jnp.where(lane == 0, total, jnp.where(lane == 1, attract, jnp.where(lane == 2, edges, entries)))
    out[...] = jnp.where(lane < 4, values, 0.0)


def finish_body(features, gathered, local_ref, pulls, row_sums, gradient, loss):
    summed = jnp.sum(gathered[...], axis=0, keepdims=True)
    lane = lax.broadcasted_iota(jnp.int32, summed.shape, 1)

    def pick(k):
        return jnp.sum(jnp.where(lane == k, summed, 0.0), axis=1, keepdims=True)

    total, attract, edges, entries = pick(0), pick(1), pick(2), pick(3)
    loss[...] = -attract / edges + jnp.log(total / entries)
    repulsion = 2.0 * edges / total
    local = local_ref[...].astype(jnp.float32)
    rows = row_sums[0] - repulsion * row_sums[1]
    gradient[...] = (2.0 / features) * (rows * local - (pulls[0] - repulsion * pulls[1]))


def per_device(embeddings, partners, pair_kind, neighbors):
    block_rows, features = embeddings.shape
    slots, knn = neighbors.shape[:2]
    groups = lax.axis_size("wide")
    devices = groups * lax.axis_size("narrow")
    half = groups // 2
    offsets = ring_offsets(groups)
    places = len(offsets)
    place_of = {offset: place for place, offset in enumerate(offsets)}
    place_of[-half] = place_of[half]
    list_shape = jax.ShapeDtypeStruct((knn + knn % 2, block_rows), jnp.bfloat16)

    def send(value, offset):
        return lax.ppermute(value, "wide", shift_pairs(groups, offset))

    right = left = embeddings
    blocks = {}
    for step in range(1, half):
        right, left = send(right, 1), send(left, -1)
        blocks[-step], blocks[step] = right, left
    middle = block_rows // 2
    upper, lower = send(right[:middle], 1), send(left[middle:], -1)
    blocks[half] = jnp.concatenate([upper, lower], axis=0)

    *own, facts = pl.pallas_call(
        functools.partial(prepare_body, groups, offsets),
        out_shape=[list_shape] * places + [jax.ShapeDtypeStruct((1, places + 2), jnp.int32)],
        in_specs=[SMEM, SMEM, VMEM],
        out_specs=[VMEM] * places + [SMEM],
        compiler_params=params(8),
    )(partners, pair_kind, neighbors)
    incoming = [None] * places
    for place, offset in enumerate(offsets):
        incoming[place_of[-offset]] = send(own[place], offset)
    counts = pl.pallas_call(
        functools.partial(counts_body, places, knn),
        out_shape=jax.ShapeDtypeStruct((places, block_rows, block_rows), jnp.bfloat16),
        in_specs=[VMEM] * (2 * places),
        out_specs=VMEM,
        compiler_params=params(16),
    )(*own, *incoming)

    state = None
    shapes = [
        jax.ShapeDtypeStruct((2, block_rows, features), jnp.float32),
        jax.ShapeDtypeStruct((2, block_rows, 1), jnp.float32),
        jax.ShapeDtypeStruct((2, 1, block_rows), jnp.float32),
    ]
    for step in range(1, half + 1):
        held = [-step, step] if step < half else [half]
        first = state is None
        operands = [facts, embeddings, counts] + [blocks[k] for k in held]
        aliases = {}
        if not first:
            aliases = {len(operands) + k: k for k in range(3)}
            operands += state
        state = pl.pallas_call(
            functools.partial(step_body, [place_of[k] for k in held], features, first),
            out_shape=shapes,
            in_specs=[SMEM] + [VMEM] * (len(operands) - 1),
            out_specs=[VMEM] * 3,
            input_output_aliases=aliases,
            compiler_params=params(16),
        )(*operands)
    pulls, row_sums, sums = state
    row = pl.pallas_call(
        functools.partial(totals_body, places, knn, block_rows),
        out_shape=jax.ShapeDtypeStruct((1, 128), jnp.float32),
        in_specs=[SMEM, VMEM],
        out_specs=VMEM,
        compiler_params=params(8),
    )(facts, sums)
    gathered = lax.all_to_all(jnp.broadcast_to(row, (devices, 128)), AXES, 0, 0, tiled=True)
    gradient, loss = pl.pallas_call(
        functools.partial(finish_body, features),
        out_shape=[
            jax.ShapeDtypeStruct((block_rows, features), jnp.float32),
            jax.ShapeDtypeStruct((1, 1), jnp.float32),
        ],
        in_specs=[VMEM] * 4,
        out_specs=[VMEM] * 2,
        compiler_params=params(16),
    )(gathered, embeddings, pulls, row_sums)
    return gradient, loss.reshape(())


def solution(mesh):
    in_specs = (P(AXES, None), P(AXES, None), P(AXES, None), P(None, None, AXES))
    return jax.shard_map(
        per_device, mesh=mesh, in_specs=in_specs, out_specs=(P(AXES, None), P()), check_vma=False
    )
```

```python
import functools

import jax
import jax.numpy as jnp
from jax import lax
from jax.experimental import pallas as pl
from jax.experimental.pallas import tpu as pltpu
from jax.sharding import PartitionSpec as P


AXES = ("wide", "narrow")
VMEM = pl.BlockSpec(memory_space=pltpu.VMEM)
SMEM = pl.BlockSpec(memory_space=pltpu.SMEM)


def ring_position(index, groups):
    return jnp.where(index % 2 == 0, index // 2, groups - 1 - index // 2)


def ring_index(position, groups):
    return jnp.where(position < groups // 2, 2 * position, 2 * (groups - position) - 1)


def ring_order(groups):
    half = groups // 2
    return [2 * q if q < half else 2 * (groups - q) - 1 for q in range(groups)]


def shift_pairs(groups, offset):
    order = ring_order(groups)
    return [(order[q], order[(q + offset) % groups]) for q in range(groups)]


def ring_offsets(groups):
    half = groups // 2
    offsets = []
    for step in range(1, half):
        offsets += [step, -step]
    return offsets + [half]


def list_rows(knn):
    return (knn // 16 + 1) * 16


def tail_groups(groups):
    half = groups // 2
    return [(a, a + 1) for a in range(half - 3, 0, -2)]


def list_spot(groups, distance, block_rows, pad):
    half = groups // 2
    if distance >= half - 1:
        return 0, (distance - half + 1) * block_rows
    for group, (near, far) in enumerate(tail_groups(groups)):
        if distance in (near, far):
            return pad * (group + 1), (distance - near) * block_rows
    raise ValueError


def compiler_params(mib):
    return pltpu.CompilerParams(vmem_limit_bytes=mib << 20)


def cost(microseconds):
    return pl.CostEstimate(
        flops=int(microseconds * 8e8), bytes_accessed=int(microseconds * 2e6), transcendentals=0
    )


def prepare_body(groups, offsets, *refs):
    inputs, (right, left, own, facts) = refs[:3], refs[3:7]
    partners, marks, neighbors, sems = refs[7:]
    copies = [
        pltpu.make_async_copy(source, held, sems.at[k])
        for k, (source, held) in enumerate(zip(inputs, (partners, marks, neighbors)))
    ]
    for copy in copies:
        copy.start()
    for copy in copies:
        copy.wait()
    knn, block_rows = neighbors.shape[1:]
    pad = own.shape[1]
    half = groups // 2
    me = ring_position(lax.axis_index("wide"), groups)
    slots = partners.shape[1]
    marked_total = jnp.int32(0)
    present_total = jnp.int32(0)
    for place, offset in enumerate(offsets):
        target = ring_index(lax.rem(me + offset + groups, groups), groups)
        slot = jnp.int32(0)
        present = jnp.int32(0)
        marked = jnp.int32(0)
        for s in range(slots):
            hit = (partners[0, s] == target).astype(jnp.int32)
            slot += hit * s
            present += hit
            marked += hit * marks[0, s]
        marked_total += marked
        present_total += present
        rows = jnp.where(marked > 0, neighbors[slot], block_rows).astype(jnp.float32)
        flag = jnp.full((pad - knn, block_rows), present.astype(jnp.float32))
        entry = jnp.concatenate([rows, flag], axis=0).astype(jnp.bfloat16)
        own[place] = entry
        row, column = list_spot(groups, abs(offset), block_rows, pad)
        for message in (right, left) if offset == half else (right,) if offset > 0 else (left,):
            message[row : row + pad, column : column + block_rows] = entry
    facts[0, 0] = present_total
    facts[0, 1] = marked_total


def join_body(pad, right_block, left_block, right_lists, left_lists, right, left):
    block_rows = right_block.shape[0]
    for block, lists, out in ((right_block, right_lists, right), (left_block, left_lists, left)):
        out[0:pad, :] = lists[0:pad, :]
        out[pad : pad + block_rows, :] = block[...]
        kept = out.shape[0] - block_rows
        if kept > pad:
            out[pad + block_rows :, :] = lists[pad:kept, :]


def histogram(entry, knn, block_rows):
    width = 4 if knn < 16 else 8
    per = 32 // width
    shift = {4: 3, 8: 2}[width]
    value = entry.astype(jnp.float32).astype(jnp.int32)
    word = value >> shift
    bit = jnp.left_shift(jnp.int32(1), (value & (per - 1)) * width)
    words = block_rows // per
    index = lax.broadcasted_iota(jnp.int32, (words, block_rows), 0)
    total = jnp.zeros((words, block_rows), jnp.int32)
    for k in range(knn):
        total += jnp.where(word[k : k + 1, :] == index, bit[k : k + 1, :], 0)
    amount = (lax.broadcasted_iota(jnp.int32, (words, per, block_rows), 1)) * width
    spread = jnp.broadcast_to(total[:, None, :], (words, per, block_rows))
    counts = lax.shift_right_logical(spread, amount) & ((1 << width) - 1)
    return counts.reshape(block_rows, block_rows)


def own_counts_body(knn, own, out):
    block_rows = out.shape[1]
    for place in range(out.shape[0]):
        counts = histogram(own[place], knn, block_rows)
        out[place] = counts.astype(jnp.float32).astype(out.dtype)


def split(weight):
    high = weight.astype(jnp.bfloat16)
    return high, (weight - high.astype(jnp.float32)).astype(jnp.bfloat16)


NT = (((1,), (1,)), ((), ()))


def rows_of(refs, pieces):
    parts = [refs[k][a:b, :] for k, a, b in pieces]
    return parts[0] if len(parts) == 1 else jnp.concatenate(parts, axis=0)


def entry_of(refs, spot, pad, block_rows):
    k, row, column = spot
    return refs[k][row : row + pad, column : column + block_rows]


def norms_column(value, scale):
    wide = value.astype(jnp.float32)
    return jnp.sum(wide * wide, axis=1, keepdims=True) * scale


def norms_row(value, scale):
    wide = value.astype(jnp.float32)
    high, low = split(wide * wide)
    ones = jnp.ones((8, value.shape[1]), jnp.bfloat16)
    total = lax.dot_general(ones, high, NT, preferred_element_type=jnp.float32)
    total += lax.dot_general(ones, low, NT, preferred_element_type=jnp.float32)
    return total[0:1, :] * scale


def transposed(counts):
    rows = counts.shape[0]
    row = lax.broadcasted_iota(jnp.int32, (rows, rows), 0)
    column = lax.broadcasted_iota(jnp.int32, (rows, rows), 1)
    identity = jnp.where(row == column, 1.0, 0.0).astype(jnp.bfloat16)
    return lax.dot_general(identity, counts, NT, preferred_element_type=jnp.float32)


CHUNK = 32


def step_body(tiles, pairs, last_sums, constants, counted, first, *refs):
    features, knn, pad = constants
    facts, local_ref, own_ref = refs[:3]
    inputs = 3 if counted else 2
    tail = inputs + 1
    held_in = [] if first else refs[-tail - inputs : -tail]
    held = refs[-tail:-1]
    weights = refs[-1]
    sources = refs[3 : len(refs) - tail - (0 if first else inputs)]
    pulls, row_sums = held[:2]
    local = local_ref[...]
    block_rows = local.shape[0]
    scale = 1.0 / features
    local_norms = 1.0 + norms_column(local, scale)
    kernel_sum = jnp.zeros((8, block_rows), jnp.float32)
    attract_sum = jnp.zeros((8, block_rows), jnp.float32)

    def fold(value):
        return jnp.sum(value.reshape(CHUNK // 8, 8, block_rows), axis=0)

    for number, (place, pieces, spot) in enumerate(tiles):
        remote = rows_of(sources, pieces)
        entry = entry_of(sources, spot, pad, block_rows)
        back = histogram(entry, knn, block_rows).astype(jnp.float32)
        counts = transposed(own_ref[place]) + back
        present = entry.astype(jnp.float32)[knn : knn + 1, :]
        remote_norms = norms_row(remote, scale)
        inner = lax.dot_general(local, remote, NT, preferred_element_type=jnp.float32)
        for start in range(0, block_rows, CHUNK):
            rows = slice(start, start + CHUNK)
            ratio = local_norms[rows] + remote_norms - inner[rows] * (2.0 * scale)
            kernel = present / ratio
            near = counts[rows] * kernel
            far = kernel * kernel
            if counted:
                kernel_sum += fold(kernel)
                attract_sum += fold(counts[rows] * jnp.log(ratio))
            for k, weight in enumerate((near, far)):
                total = jnp.sum(weight, axis=1, keepdims=True)
                if number:
                    total += row_sums[k, rows, :]
                elif not first:
                    total += held_in[1][k, rows, :]
                row_sums[k, rows, :] = total
                high, low = split(weight)
                weights[2 * k, rows, :] = high
                weights[2 * k + 1, rows, :] = low
        for k in range(2):
            product = jnp.dot(weights[2 * k], remote, preferred_element_type=jnp.float32)
            product += jnp.dot(weights[2 * k + 1], remote, preferred_element_type=jnp.float32)
            if number:
                product += pulls[k]
            elif not first:
                product += held_in[0][k]
            pulls[k] = product
    for left_pieces, right_pieces, there, back_spot, weight in pairs:
        left, right = rows_of(sources, left_pieces), rows_of(sources, right_pieces)
        entry = entry_of(sources, there, pad, block_rows)
        forward = histogram(entry, knn, block_rows).astype(jnp.float32).astype(jnp.bfloat16)
        entry = entry_of(sources, back_spot, pad, block_rows)
        counts = transposed(forward) + histogram(entry, knn, block_rows).astype(jnp.float32)
        present = entry.astype(jnp.float32)[knn : knn + 1, :] * weight
        left_norms = 1.0 + norms_column(left, scale)
        right_norms = norms_row(right, scale)
        inner = lax.dot_general(left, right, NT, preferred_element_type=jnp.float32)
        for start in range(0, block_rows, CHUNK):
            rows = slice(start, start + CHUNK)
            ratio = left_norms[rows] + right_norms - inner[rows] * (2.0 * scale)
            kernel_sum += fold(present / ratio)
            attract_sum += fold((weight * counts[rows]) * jnp.log(ratio))
    if not counted:
        return
    if not first:
        kernel_sum += held_in[2][0]
        attract_sum += held_in[2][1]
    sums = held[2]
    if not last_sums:
        sums[0] = kernel_sum
        sums[1] = attract_sum
        return
    lane = lax.broadcasted_iota(jnp.int32, sums.shape, 1)
    values = (
        jnp.sum(kernel_sum),
        jnp.sum(attract_sum) * -0.5,
        facts[0, 1].astype(jnp.float32) * float(knn * block_rows),
        facts[0, 0].astype(jnp.float32) * float(block_rows * block_rows),
    )
    row = jnp.zeros(sums.shape, jnp.float32)
    for k, value in enumerate(values):
        row = jnp.where(lane == k, value, row)
    sums[...] = row


def finish_body(groups, features, table, center_ref, *refs):
    windows = refs[: len(table) - 1]
    local_ref, pulls, row_sums, gradient, loss, relative = refs[len(table) - 1 :]
    sources = (center_ref,) + windows
    for ref, rows in zip(sources, table):
        for row, offset in rows:
            relative[offset : offset + 1, :] = ref[row : row + 1, :]
    me = ring_position(lax.axis_index("wide"), groups)
    summed = jnp.sum(pltpu.roll(relative[...], me, 0), axis=0, keepdims=True)
    lane = lax.broadcasted_iota(jnp.int32, summed.shape, 1)

    def pick(k):
        return jnp.sum(jnp.where(lane == k, summed, 0.0), axis=1, keepdims=True)

    total, attract, edges, entries = pick(0), pick(1), pick(2), pick(3)
    loss[...] = -attract / edges + jnp.log(total / entries)
    repulsion = 2.0 * edges / total
    local = local_ref[...].astype(jnp.float32)
    rows = row_sums[0] - repulsion * row_sums[1]
    gradient[...] = (2.0 / features) * (rows * local - (pulls[0] - repulsion * pulls[1]))


def column_step(embeddings, partners, pair_kind, neighbors):
    block_rows, features = embeddings.shape
    knn = neighbors.shape[1]
    pad = list_rows(knn)
    groups = lax.axis_size("wide")
    half, quarter = groups // 2, groups // 4
    offsets = ring_offsets(groups)
    places = len(offsets)
    place_of = {offset: place for place, offset in enumerate(offsets)}
    tails = tail_groups(groups)
    list_height = pad * (len(tails) + 1)
    lists = jax.ShapeDtypeStruct((list_height, features), embeddings.dtype)

    def send(value, offset):
        return lax.ppermute(value, "wide", shift_pairs(groups, offset))

    def both(right, left):
        return [send(right, 1), send(left, -1)]

    def height(step):
        return pad * (1 + sum(far >= step for _, far in tails))

    blocks = both(embeddings, embeddings)
    right, left, own, facts = pl.pallas_call(
        functools.partial(prepare_body, groups, offsets),
        out_shape=[
            lists,
            lists,
            jax.ShapeDtypeStruct((places, pad, block_rows), jnp.bfloat16),
            jax.ShapeDtypeStruct((1, 2), jnp.int32),
        ],
        in_specs=[pl.BlockSpec(memory_space=pltpu.HBM)] * 3,
        out_specs=[VMEM, VMEM, VMEM, SMEM],
        scratch_shapes=[
            pltpu.SMEM(partners.shape, jnp.int32),
            pltpu.SMEM(pair_kind.shape, jnp.int32),
            pltpu.VMEM(neighbors.shape, jnp.int32),
            pltpu.SemaphoreType.DMA((3,)),
        ],
        compiler_params=compiler_params(8),
        cost_estimate=cost(1.5),
        name="prepare",
    )(*(pltpu.with_memory_space_constraint(x, pltpu.HBM) for x in (partners, pair_kind, neighbors)))
    notes = both(right, left)
    own_counts = pl.pallas_call(
        functools.partial(own_counts_body, knn),
        out_shape=jax.ShapeDtypeStruct((places, block_rows, block_rows), jnp.bfloat16),
        in_specs=[VMEM],
        out_specs=VMEM,
        compiler_params=compiler_params(8),
        cost_estimate=cost(1.0),
        name="own_counts",
    )(own)
    arrived = {1: blocks + notes}
    for step in range(2, quarter + 1):
        blocks = both(*blocks)
        notes = both(*(note[: height(step)] for note in notes))
        arrived[step] = blocks + notes
    message = jax.ShapeDtypeStruct((block_rows + height(quarter + 1), features), embeddings.dtype)
    right, left = pl.pallas_call(
        functools.partial(join_body, pad),
        out_shape=[message, message],
        in_specs=[VMEM] * 4,
        out_specs=[VMEM] * 2,
        compiler_params=compiler_params(4),
        cost_estimate=cost(0.3),
        name="join",
    )(*blocks, *notes)
    for step in range(quarter + 1, half):
        keep = block_rows + height(step)
        right, left = arrived[step] = both(right[:keep], left[:keep])
    middle = pad + block_rows // 2
    arrived[half] = both(right[:middle], left[middle : pad + block_rows])

    def spot_of(step, side, distance):
        row, column = list_spot(groups, distance, block_rows, pad)
        if step <= quarter:
            return side + 2, row, column
        return side, row + (block_rows if row else 0), column

    def block_of(step, side):
        start = 0 if step <= quarter else pad
        return [(side, start, start + block_rows)]

    state = None
    constants = (features, knn, pad)
    for step in range(1, half + 1):
        counted = step <= quarter
        sources = list(arrived[step])
        if step < half:
            tiles = [
                (place_of[-step], block_of(step, 0), spot_of(step, 0, step)),
                (place_of[step], block_of(step, 1), spot_of(step, 1, step)),
            ]
        else:
            pieces = [(0, pad, middle), (1, 0, block_rows // 2)]
            tiles = [(place_of[half], pieces, spot_of(step, 0, half))]
        pairs = []
        if step == quarter:
            for distance in range(quarter + 1, half + 1):
                lower = distance - quarter
                at, factor = 0, 1.0
                there = spot_of(step, 0, distance)
                if lower != quarter:
                    at, factor = len(sources), 2.0
                    sources += [arrived[lower][0], arrived[lower][2]]
                    there = (at + 1,) + there[1:]
                pairs.append(
                    (block_of(step, at), block_of(step, 1), there, spot_of(step, 1, distance), factor)
                )
        first = state is None
        operands = [facts, embeddings, own_counts] + sources
        shapes = [
            jax.ShapeDtypeStruct((2, block_rows, features), jnp.float32),
            jax.ShapeDtypeStruct((2, block_rows, 1), jnp.float32),
        ]
        if step == quarter:
            shapes.append(jax.ShapeDtypeStruct((1, 128), jnp.float32))
        elif counted:
            shapes.append(jax.ShapeDtypeStruct((2, 8, block_rows), jnp.float32))
        aliases = {}
        if not first:
            aliases = {len(operands) + k: k for k in range(2)}
            operands += state
        state = pl.pallas_call(
            functools.partial(step_body, tiles, pairs, step == quarter, constants, counted, first),
            out_shape=shapes,
            in_specs=[SMEM] + [VMEM] * (len(operands) - 1),
            out_specs=[VMEM] * len(shapes),
            scratch_shapes=[pltpu.VMEM((4, block_rows, block_rows), jnp.bfloat16)],
            input_output_aliases=aliases,
            compiler_params=compiler_params(12),
            cost_estimate=cost(1.0 * len(tiles) + 0.6 * len(pairs)),
        )(*operands)
        if step == quarter:
            window, *_ = state[2:]
            state = state[:2]
    columns = lax.axis_size("narrow")
    bit = 1
    while bit < columns:
        other = lax.ppermute(window, "narrow", [(k, k ^ bit) for k in range(columns)])
        window = window + other
        bit *= 2
    reach, received = 0, []
    table = [[(0, 0)]]
    while 2 * reach + 1 < groups:
        if reach:
            window = jnp.concatenate([received[1], window, received[0]], axis=0)
            table = [[(row, (row - reach) % groups) for row in range(2 * reach + 1)]]
        stride = 2 * reach + 1
        received = [send(window, -stride), send(window, stride)]
        seen = {offset for _, offset in table[0]}
        for sign in (1, -1):
            rows = []
            for row in range(2 * reach + 1):
                offset = (sign * stride + row - reach) % groups
                if offset not in seen:
                    seen.add(offset)
                    rows.append((row, offset))
            table.append(rows)
        reach = 3 * reach + 1
    gradient, loss = pl.pallas_call(
        functools.partial(finish_body, groups, features, table),
        out_shape=[
            jax.ShapeDtypeStruct((block_rows, features), jnp.float32),
            jax.ShapeDtypeStruct((1, 1), jnp.float32),
        ],
        in_specs=[VMEM] * (3 + len(table)),
        out_specs=[VMEM] * 2,
        scratch_shapes=[pltpu.VMEM((groups, 128), jnp.float32)],
        compiler_params=compiler_params(12),
        cost_estimate=cost(1.0),
        name="finish",
    )(window, *received, embeddings, *state)
    return gradient, loss.reshape(())


def solution(mesh):
    in_specs = (P(AXES, None), P(AXES, None), P(AXES, None), P(None, None, AXES))
    return jax.shard_map(
        column_step, mesh=mesh, in_specs=in_specs, out_specs=(P(AXES, None), P()), check_vma=False
    )
```

```python
import functools

import jax
import jax.numpy as jnp
from jax import lax
from jax.experimental import pallas as pl
from jax.experimental.pallas import tpu as pltpu
from jax.sharding import PartitionSpec as P


AXES = ("wide", "narrow")
VMEM = pl.BlockSpec(memory_space=pltpu.VMEM)
SMEM = pl.BlockSpec(memory_space=pltpu.SMEM)


def ring_position(index, groups):
    return jnp.where(index % 2 == 0, index // 2, groups - 1 - index // 2)


def ring_index(position, groups):
    return jnp.where(position < groups // 2, 2 * position, 2 * (groups - position) - 1)


def ring_order(groups):
    half = groups // 2
    return [2 * q if q < half else 2 * (groups - q) - 1 for q in range(groups)]


def shift_pairs(groups, offset):
    order = ring_order(groups)
    return [(order[q], order[(q + offset) % groups]) for q in range(groups)]


def ring_offsets(groups):
    half = groups // 2
    offsets = []
    for step in range(1, half):
        offsets += [step, -step]
    return offsets + [half]


def list_rows(knn):
    return (knn // 16 + 1) * 16


def tail_groups(groups):
    half = groups // 2
    return [(a, a + 1) for a in range(half - 3, 0, -2)]


def list_spot(groups, distance, block_rows, pad):
    half = groups // 2
    if distance >= half - 1:
        return 0, (distance - half + 1) * block_rows
    for group, (near, far) in enumerate(tail_groups(groups)):
        if distance in (near, far):
            return pad * (group + 1), (distance - near) * block_rows
    raise ValueError


def compiler_params(mib):
    return pltpu.CompilerParams(vmem_limit_bytes=mib << 20)


def cost(microseconds):
    return pl.CostEstimate(
        flops=int(microseconds * 8e8), bytes_accessed=int(microseconds * 2e6), transcendentals=0
    )


def prepare_body(groups, offsets, *refs):
    inputs, (right, left, own, base, local) = refs[:4], refs[4:9]
    partners, marks, neighbors, sems = refs[9:]
    copies = [
        pltpu.make_async_copy(source, held, sems.at[k])
        for k, (source, held) in enumerate(zip(inputs, (partners, marks, neighbors, local)))
    ]
    for copy in copies:
        copy.start()
    for copy in copies[:3]:
        copy.wait()
    knn, block_rows = neighbors.shape[1:]
    pad = own.shape[1]
    half = groups // 2
    me = ring_position(lax.axis_index("wide"), groups)
    slots = partners.shape[1]
    marked_total = jnp.int32(0)
    present_total = jnp.int32(0)
    for place, offset in enumerate(offsets):
        target = ring_index(lax.rem(me + offset + groups, groups), groups)
        slot = jnp.int32(0)
        present = jnp.int32(0)
        marked = jnp.int32(0)
        for s in range(slots):
            hit = (partners[0, s] == target).astype(jnp.int32)
            slot += hit * s
            present += hit
            marked += hit * marks[0, s]
        marked_total += marked
        present_total += present
        empty = jnp.where(present > 0, block_rows, 2 * block_rows)
        rows = jnp.where(marked > 0, neighbors[slot], empty).astype(jnp.float32)
        filler = jnp.zeros((pad - knn, block_rows), jnp.float32)
        entry = jnp.concatenate([rows, filler], axis=0).astype(jnp.bfloat16)
        own[place] = entry
        row, column = list_spot(groups, abs(offset), block_rows, pad)
        for message in (right, left) if offset == half else (right,) if offset > 0 else (left,):
            message[row : row + pad, column : column + block_rows] = entry
    lane = lax.broadcasted_iota(jnp.int32, base.shape, 1)
    edges = marked_total.astype(jnp.float32) * float(knn * block_rows)
    entries = present_total.astype(jnp.float32) * float(block_rows * block_rows)
    base[...] = jnp.where(lane == 2, edges, jnp.where(lane == 3, entries, 0.0))
    copies[3].wait()
    wide = local[...].astype(jnp.float32)
    high, low = split(wide * wide)
    ones = jnp.ones((8, wide.shape[1]), jnp.bfloat16)
    norms = lax.dot_general(ones, high, NT, preferred_element_type=jnp.float32)
    norms += lax.dot_general(ones, low, NT, preferred_element_type=jnp.float32)
    for message in (right, left):
        for k, part in enumerate(split(norms[0:1, :])):
            message[knn : knn + 1, k * block_rows : (k + 1) * block_rows] = part


def join_body(pad, right_block, left_block, right_lists, left_lists, right, left):
    block_rows = right_block.shape[0]
    for block, lists, out in ((right_block, right_lists, right), (left_block, left_lists, left)):
        out[0:pad, :] = lists[0:pad, :]
        out[pad : pad + block_rows, :] = block[...]
        kept = out.shape[0] - block_rows
        if kept > pad:
            out[pad + block_rows :, :] = lists[pad:kept, :]


def histogram(entry, knn, block_rows):
    width = 4 if knn < 16 else 8
    per = 32 // width
    shift = {4: 3, 8: 2}[width]
    value = entry.astype(jnp.float32).astype(jnp.int32)
    word = value >> shift
    bit = jnp.left_shift(jnp.int32(1), (value & (per - 1)) * width)
    words = block_rows // per
    index = lax.broadcasted_iota(jnp.int32, (words, block_rows), 0)
    total = jnp.zeros((words, block_rows), jnp.int32)
    for k in range(knn):
        total += jnp.where(word[k : k + 1, :] == index, bit[k : k + 1, :], 0)
    amount = (lax.broadcasted_iota(jnp.int32, (words, per, block_rows), 1)) * width
    spread = jnp.broadcast_to(total[:, None, :], (words, per, block_rows))
    counts = lax.shift_right_logical(spread, amount) & ((1 << width) - 1)
    return counts.reshape(block_rows, block_rows)


def own_counts_body(knn, own, out):
    block_rows = out.shape[1]
    for place in range(out.shape[0]):
        counts = histogram(own[place], knn, block_rows)
        out[place] = counts.astype(jnp.float32).astype(out.dtype)


def split(weight):
    high = weight.astype(jnp.bfloat16)
    return high, (weight - high.astype(jnp.float32)).astype(jnp.bfloat16)


NT = (((1,), (1,)), ((), ()))


def rows_of(refs, pieces):
    parts = [refs[k][a:b, :] for k, a, b in pieces]
    return parts[0] if len(parts) == 1 else jnp.concatenate(parts, axis=0)


def entry_of(refs, spot, pad, block_rows):
    k, row, column = spot
    return refs[k][row : row + pad, column : column + block_rows]


def identity_of(rows):
    row = lax.broadcasted_iota(jnp.int32, (rows, rows), 0)
    column = lax.broadcasted_iota(jnp.int32, (rows, rows), 1)
    return jnp.where(row == column, 1.0, 0.0).astype(jnp.bfloat16)


def transposed(counts):
    return lax.dot_general(identity_of(counts.shape[0]), counts, NT, preferred_element_type=jnp.float32)


def norm_parts(message, knn, block_rows):
    row = message[knn : knn + 1, :].astype(jnp.float32)
    return row[:, :block_rows], row[:, block_rows:]


def norm_table(parts, features, mine):
    high = float(features >> max(features.bit_length() - 8, 0) << max(features.bit_length() - 8, 0))
    fixed = (1.0, 1.0, high, features - high) if mine else (1.0, 1.0, 1.0, 1.0)
    own_first = 0 if mine else 2
    block_rows = parts[0].shape[1]
    row = lax.broadcasted_iota(jnp.int32, (16, block_rows), 0)
    table = jnp.zeros((16, block_rows), jnp.float32)
    for k, value in ((2 - own_first, fixed[0]), (3 - own_first, fixed[1]), (4, fixed[2]), (5, fixed[3])):
        table = jnp.where(row == k, value, table)
    for k, part in enumerate(parts):
        table = jnp.where(row == own_first + k, part, table)
    return table.astype(jnp.bfloat16)


TN = (((0,), (0,)), ((), ()))
CHUNK = 32


def fold(value):
    rows, lanes = value.shape
    return jnp.sum(value.reshape(rows // 8, 8, lanes), axis=0)


def kernel_phase(a, a_norms, b, b_norms, present, counts, constants, out, totals, weight=1.0):
    features = constants[0]
    base = lax.dot_general(
        norm_table(a_norms, features, True),
        norm_table(b_norms, features, False),
        TN,
        preferred_element_type=jnp.float32,
    )
    inner = lax.dot_general(a * -2.0, b, NT, preferred_element_type=jnp.float32)
    block_rows = a.shape[0]
    for start in range(0, block_rows, CHUNK):
        rows = slice(start, start + CHUNK)
        scaled = base[rows] + inner[rows]
        kernel = (present * (features * weight)) / scaled
        if out is not None:
            out[rows, :] = kernel
        if totals is not None:
            logs = jnp.log(scaled * (1.0 / features))
            totals[0] += fold(kernel)
            totals[1] += fold((weight * counts[rows]) * logs)


def pull_phase(remote, kernel, counts, weights, pulls_in, rows_in, pulls, row_sums):
    block_rows = remote.shape[0]
    for start in range(0, block_rows, CHUNK):
        rows = slice(start, start + CHUNK)
        value = kernel[rows, :]
        near = counts[rows, :].astype(jnp.float32) * value
        far = value * value
        for k, weight in enumerate((near, far)):
            total = jnp.sum(weight, axis=1, keepdims=True)
            if rows_in is not None:
                total += rows_in[k, rows, :]
            row_sums[k, rows, :] = total
        high, low = split(near)
        for k, part in enumerate((high, low, far.astype(jnp.bfloat16))):
            weights[k * block_rows + start : k * block_rows + start + CHUNK, :] = part
    product = jnp.dot(weights[...], remote, preferred_element_type=jnp.float32)
    near = product[:block_rows] + product[block_rows : 2 * block_rows]
    far = product[2 * block_rows :]
    pulls[0] = near if pulls_in is None else near + pulls_in[0]
    pulls[1] = far if pulls_in is None else far + pulls_in[1]


def tile_counts(own, entry, knn):
    back = histogram(entry, knn, own.shape[0]).astype(jnp.float32)
    present = jnp.where(entry[0:1, :].astype(jnp.float32) <= float(own.shape[0]), 1.0, 0.0)
    return transposed(own) + back, present


def step_body(tiles, counted, first, constants, *refs):
    _, knn, pad = constants
    local_ref, note_ref, own_ref = refs[:3]
    kernel, weights = refs[-2:]
    held_count = 3 if counted else 2
    held = refs[-2 - held_count : -2]
    held_in = [None] * 3 if first else refs[-2 - 2 * held_count : -2 - held_count]
    sources = refs[3 : len(refs) - 2 - held_count * (1 if first else 2)]
    local = local_ref[...]
    block_rows = local.shape[0]
    local_norms = norm_parts(note_ref, knn, block_rows)
    totals = None
    if counted:
        if first:
            zero = jnp.zeros((8, block_rows), jnp.float32)
            totals = [zero, zero]
        else:
            totals = [held_in[2][0], held_in[2][1]]
    for number, (place, pieces, front, spot) in enumerate(tiles):
        remote = rows_of(sources, pieces)
        entry = entry_of(sources, spot, pad, block_rows)
        counts, present = tile_counts(own_ref[place], entry, knn)
        remote_norms = norm_parts(sources[front], knn, block_rows)
        kernel_phase(local, local_norms, remote, remote_norms, present, counts, constants, kernel, totals)
        before = held if number else held_in
        pull_phase(remote, kernel, counts, weights, before[0], before[1], held[0], held[1])
    if counted:
        held[2][0] = totals[0]
        held[2][1] = totals[1]


def sums_body(tiles, pairs, constants, *refs):
    _, knn, pad = constants
    local_ref, note_ref, own_ref, base_ref, sums_in = refs[:5]
    row_ref, kernels, all_counts = refs[-3:]
    sources = refs[5:-3]
    local = local_ref[...]
    block_rows = local.shape[0]
    local_norms = norm_parts(note_ref, knn, block_rows)
    totals = [sums_in[0], sums_in[1]]
    for number, (place, pieces, front, spot) in enumerate(tiles):
        remote = rows_of(sources, pieces)
        entry = entry_of(sources, spot, pad, block_rows)
        counts, present = tile_counts(own_ref[place], entry, knn)
        all_counts[number] = counts.astype(all_counts.dtype)
        remote_norms = norm_parts(sources[front], knn, block_rows)
        kernel_phase(
            local, local_norms, remote, remote_norms, present, counts, constants, kernels.at[number], totals
        )
    for left_pieces, left_front, right_pieces, right_front, there, back, weight in pairs:
        entry = entry_of(sources, there, pad, block_rows)
        forward = histogram(entry, knn, block_rows).astype(jnp.float32).astype(jnp.bfloat16)
        counts, present = tile_counts(forward, entry_of(sources, back, pad, block_rows), knn)
        kernel_phase(
            rows_of(sources, left_pieces),
            norm_parts(sources[left_front], knn, block_rows),
            rows_of(sources, right_pieces),
            norm_parts(sources[right_front], knn, block_rows),
            present,
            counts,
            constants,
            None,
            totals,
            weight,
        )
    lane = lax.broadcasted_iota(jnp.int32, row_ref.shape, 1)
    row = jnp.where(lane == 0, jnp.sum(totals[0]), base_ref[...])
    row_ref[...] = jnp.where(lane == 1, jnp.sum(totals[1]) * -0.5, row)


def pull_body(tiles, *refs):
    kernels, counts = refs[:2]
    pulls_in, rows_in, pulls, row_sums, weights = refs[-5:]
    sources = refs[2:-5]
    for number, (_, pieces, _, _) in enumerate(tiles):
        before = (pulls, row_sums) if number else (pulls_in, rows_in)
        pull_phase(
            rows_of(sources, pieces), kernels.at[number], counts.at[number], weights, *before, pulls, row_sums
        )


def finish_body(groups, features, table, *refs):
    windows = refs[: len(table)]
    local_ref, pulls, row_sums, gradient, loss, relative = refs[len(table) :]
    for ref, rows in zip(windows, table):
        for row, offset in rows:
            relative[offset : offset + 1, :] = ref[row : row + 1, :]
    me = ring_position(lax.axis_index("wide"), groups)
    summed = jnp.sum(pltpu.roll(relative[...], me, 0), axis=0, keepdims=True)
    lane = lax.broadcasted_iota(jnp.int32, summed.shape, 1)

    def pick(k):
        return jnp.sum(jnp.where(lane == k, summed, 0.0), axis=1, keepdims=True)

    total, attract, edges, entries = pick(0), pick(1), pick(2), pick(3)
    loss[...] = -attract / edges + jnp.log(total / entries)
    repulsion = 2.0 * edges / total
    scale = 2.0 / features
    near_scale, far_scale = scale, scale * repulsion
    for start in range(0, gradient.shape[0], CHUNK):
        chunk = slice(start, start + CHUNK)
        rows = near_scale * row_sums[0, chunk, :] - far_scale * row_sums[1, chunk, :]
        pull = near_scale * pulls[0, chunk, :] - far_scale * pulls[1, chunk, :]
        gradient[chunk, :] = rows * local_ref[chunk, :].astype(jnp.float32) - pull


def column_step(embeddings, partners, pair_kind, neighbors):
    block_rows, features = embeddings.shape
    knn = neighbors.shape[1]
    pad = list_rows(knn)
    groups = lax.axis_size("wide")
    half, quarter = groups // 2, groups // 4
    offsets = ring_offsets(groups)
    places = len(offsets)
    place_of = {offset: place for place, offset in enumerate(offsets)}
    tails = tail_groups(groups)
    list_height = pad * (len(tails) + 1)
    lists = jax.ShapeDtypeStruct((list_height, features), embeddings.dtype)

    def send(value, offset):
        return lax.ppermute(value, "wide", shift_pairs(groups, offset))

    def both(right, left):
        return [send(right, 1), send(left, -1)]

    def height(step):
        return pad * (1 + sum(far >= step for _, far in tails))

    blocks = both(embeddings, embeddings)
    right_note, left_note, own, base, local = pl.pallas_call(
        functools.partial(prepare_body, groups, offsets),
        out_shape=[
            lists,
            lists,
            jax.ShapeDtypeStruct((places, pad, block_rows), jnp.bfloat16),
            jax.ShapeDtypeStruct((1, 128), jnp.float32),
            jax.ShapeDtypeStruct(embeddings.shape, embeddings.dtype),
        ],
        in_specs=[pl.BlockSpec(memory_space=pltpu.HBM)] * 4,
        out_specs=[VMEM] * 5,
        scratch_shapes=[
            pltpu.SMEM(partners.shape, jnp.int32),
            pltpu.SMEM(pair_kind.shape, jnp.int32),
            pltpu.VMEM(neighbors.shape, jnp.int32),
            pltpu.SemaphoreType.DMA((4,)),
        ],
        compiler_params=compiler_params(8),
        cost_estimate=cost(1.5),
        name="prepare",
    )(*(pltpu.with_memory_space_constraint(x, pltpu.HBM) for x in (partners, pair_kind, neighbors, embeddings)))
    notes = both(right_note, left_note)
    own_counts = pl.pallas_call(
        functools.partial(own_counts_body, knn),
        out_shape=jax.ShapeDtypeStruct((places, block_rows, block_rows), jnp.bfloat16),
        in_specs=[VMEM],
        out_specs=VMEM,
        compiler_params=compiler_params(8),
        cost_estimate=cost(1.0),
        name="own_counts",
    )(own)
    arrived = {1: blocks + notes}
    for step in range(2, quarter + 1):
        blocks = both(*blocks)
        notes = [
            send(note[: height(step)], sign * step)
            for note, sign in ((right_note, 1), (left_note, -1))
        ]
        arrived[step] = blocks + notes
    message = jax.ShapeDtypeStruct((block_rows + height(quarter + 1), features), embeddings.dtype)
    right, left = pl.pallas_call(
        functools.partial(join_body, pad),
        out_shape=[message, message],
        in_specs=[VMEM] * 4,
        out_specs=[VMEM] * 2,
        compiler_params=compiler_params(4),
        cost_estimate=cost(0.3),
        name="join",
    )(*blocks, *notes)
    for step in range(quarter + 1, half):
        keep = block_rows + height(step)
        right, left = arrived[step] = both(right[:keep], left[:keep])
    middle = pad + block_rows // 2
    arrived[half] = both(right[:middle], left[middle : pad + block_rows])

    def spot_of(step, side, distance):
        row, column = list_spot(groups, distance, block_rows, pad)
        if step <= quarter:
            return side + 2, row, column
        return side, row + (block_rows if row else 0), column

    def block_of(step, side):
        start = 0 if step <= quarter else pad
        return [(side, start, start + block_rows)]

    def front_of(step, side):
        return side + 2 if step <= quarter else side

    def tiles_of(step):
        if step == half:
            pieces = [(0, pad, middle), (1, 0, block_rows // 2)]
            return [(place_of[half], pieces, 0, spot_of(step, 0, half))]
        return [
            (place_of[sign * step], block_of(step, side), front_of(step, side), spot_of(step, side, step))
            for side, sign in ((0, -1), (1, 1))
        ]

    def call(body, operands, shapes, time, aliases=None, scratch=()):
        return pl.pallas_call(
            body,
            out_shape=shapes,
            in_specs=[VMEM] * len(operands),
            out_specs=[VMEM] * len(shapes),
            scratch_shapes=list(scratch),
            input_output_aliases=aliases or {},
            compiler_params=compiler_params(12),
            cost_estimate=cost(time),
        )(*operands)

    constants = (features, knn, pad)
    square = (block_rows, block_rows)
    scratch = [
        pltpu.VMEM(square, jnp.float32),
        pltpu.VMEM((3 * block_rows, block_rows), jnp.bfloat16),
    ]
    held = [
        jax.ShapeDtypeStruct((2, block_rows, features), jnp.float32),
        jax.ShapeDtypeStruct((2, block_rows, 1), jnp.float32),
        jax.ShapeDtypeStruct((2, 8, block_rows), jnp.float32),
    ]
    common = [local, right_note, own_counts]
    state = None
    for step in range(1, half + 1):
        tiles = tiles_of(step)
        if step == quarter:
            sources, pairs = list(arrived[step]), []
            for distance in range(quarter + 1, half + 1):
                lower = distance - quarter
                at, front, factor = 0, 2, 1.0
                if lower != quarter:
                    at, front, factor = len(sources), len(sources) + 1, 2.0
                    sources += [arrived[lower][0], arrived[lower][2]]
                there = (front,) + spot_of(step, 0, distance)[1:]
                pairs.append(
                    (
                        block_of(step, at),
                        front,
                        block_of(step, 1),
                        3,
                        there,
                        spot_of(step, 1, distance),
                        factor,
                    )
                )
            window, kernels, counts = call(
                functools.partial(sums_body, tiles, pairs, constants),
                common + [base, state[2]] + sources,
                [
                    jax.ShapeDtypeStruct((1, 128), jnp.float32),
                    jax.ShapeDtypeStruct((2, *square), jnp.float32),
                    jax.ShapeDtypeStruct((2, *square), jnp.bfloat16),
                ],
                1.8,
            )
            operands = [kernels, counts] + arrived[step][:2]
            state = call(
                functools.partial(pull_body, tiles),
                operands + list(state[:2]),
                held[:2],
                1.5,
                {len(operands) + k: k for k in range(2)},
                scratch[1:],
            )
            continue
        counted = step < quarter
        operands = common + arrived[step]
        shapes = held if counted else held[:2]
        first = state is None
        aliases = {} if first else {len(operands) + k: k for k in range(len(shapes))}
        state = call(
            functools.partial(step_body, tiles, counted, first, constants),
            operands + ([] if first else list(state)),
            shapes,
            2.0,
            aliases,
            scratch,
        )
    columns = lax.axis_size("narrow")
    bit = 1
    while bit < columns:
        other = lax.ppermute(window, "narrow", [(k, k ^ bit) for k in range(columns)])
        window = window + other
        bit *= 2
    reach, received = 0, []
    table = [[(0, 0)]]
    while 2 * reach + 1 < groups:
        if reach:
            window = jnp.concatenate([received[1], window, received[0]], axis=0)
            table = [[(row, (row - reach) % groups) for row in range(2 * reach + 1)]]
        stride = 2 * reach + 1
        received = [send(window, -stride), send(window, stride)]
        seen = {offset for _, offset in table[0]}
        for sign in (1, -1):
            rows = []
            for row in range(2 * reach + 1):
                offset = (sign * stride + row - reach) % groups
                if offset not in seen:
                    seen.add(offset)
                    rows.append((row, offset))
            table.append(rows)
        reach = 3 * reach + 1
    gradient, loss = call(
        functools.partial(finish_body, groups, features, table),
        [window, *received, local, *state],
        [
            jax.ShapeDtypeStruct((block_rows, features), jnp.float32),
            jax.ShapeDtypeStruct((1, 1), jnp.float32),
        ],
        1.0,
        None,
        [pltpu.VMEM((groups, 128), jnp.float32)],
    )
    return gradient, loss.reshape(())


def solution(mesh):
    in_specs = (P(AXES, None), P(AXES, None), P(AXES, None), P(None, None, AXES))
    return jax.shard_map(
        column_step, mesh=mesh, in_specs=in_specs, out_specs=(P(AXES, None), P()), check_vma=False
    )
```

```python
import functools

import jax
import jax.numpy as jnp
from jax import lax
from jax.experimental import pallas as pl
from jax.experimental.pallas import tpu as pltpu
from jax.sharding import PartitionSpec as P


AXES = ("wide", "narrow")
VMEM = pl.BlockSpec(memory_space=pltpu.VMEM)
SMEM = pl.BlockSpec(memory_space=pltpu.SMEM)


def ring_position(index, groups):
    return jnp.where(index % 2 == 0, index // 2, groups - 1 - index // 2)


def ring_index(position, groups):
    return jnp.where(position < groups // 2, 2 * position, 2 * (groups - position) - 1)


def ring_order(groups):
    half = groups // 2
    return [2 * q if q < half else 2 * (groups - q) - 1 for q in range(groups)]


def shift_pairs(groups, offset):
    order = ring_order(groups)
    return [(order[q], order[(q + offset) % groups]) for q in range(groups)]


def ring_offsets(groups):
    half = groups // 2
    offsets = []
    for step in range(1, half):
        offsets += [step, -step]
    return offsets + [half]


def list_rows(knn):
    return (knn // 16 + 1) * 16


def tail_groups(groups):
    half = groups // 2
    return [(a, a + 1) for a in range(half - 3, 0, -2)]


def list_spot(groups, distance, block_rows, pad):
    half = groups // 2
    if distance >= half - 1:
        return 0, (distance - half + 1) * block_rows
    for group, (near, far) in enumerate(tail_groups(groups)):
        if distance in (near, far):
            return pad * (group + 1), (distance - near) * block_rows
    raise ValueError


def compiler_params(mib):
    return pltpu.CompilerParams(vmem_limit_bytes=mib << 20)


def cost(microseconds):
    return pl.CostEstimate(
        flops=int(microseconds * 8e8), bytes_accessed=int(microseconds * 2e6), transcendentals=0
    )


def prepare_body(groups, offsets, *refs):
    inputs, (right, left, own, base, local) = refs[:4], refs[4:9]
    partners, marks, neighbors, sems = refs[9:]
    copies = [
        pltpu.make_async_copy(source, held, sems.at[k])
        for k, (source, held) in enumerate(zip(inputs, (partners, marks, neighbors, local)))
    ]
    for copy in copies:
        copy.start()
    for copy in copies[:3]:
        copy.wait()
    knn, block_rows = neighbors.shape[1:]
    pad = own.shape[1]
    half = groups // 2
    me = ring_position(lax.axis_index("wide"), groups)
    slots = partners.shape[1]
    marked_total = jnp.int32(0)
    present_total = jnp.int32(0)
    for place, offset in enumerate(offsets):
        target = ring_index(lax.rem(me + offset + groups, groups), groups)
        slot = jnp.int32(0)
        present = jnp.int32(0)
        marked = jnp.int32(0)
        for s in range(slots):
            hit = (partners[0, s] == target).astype(jnp.int32)
            slot += hit * s
            present += hit
            marked += hit * marks[0, s]
        marked_total += marked
        present_total += present
        empty = jnp.where(present > 0, block_rows, 2 * block_rows)
        rows = jnp.where(marked > 0, neighbors[slot], empty).astype(jnp.float32)
        filler = jnp.zeros((pad - knn, block_rows), jnp.float32)
        entry = jnp.concatenate([rows, filler], axis=0).astype(jnp.bfloat16)
        own[place] = entry
        row, column = list_spot(groups, abs(offset), block_rows, pad)
        for message in (right, left) if offset == half else (right,) if offset > 0 else (left,):
            message[row : row + pad, column : column + block_rows] = entry
    lane = lax.broadcasted_iota(jnp.int32, base.shape, 1)
    edges = marked_total.astype(jnp.float32) * float(knn * block_rows)
    entries = present_total.astype(jnp.float32) * float(block_rows * block_rows)
    base[...] = jnp.where(lane == 2, edges, jnp.where(lane == 3, entries, 0.0))
    copies[3].wait()
    wide = local[...].astype(jnp.float32)
    high, low = split(wide * wide)
    ones = jnp.ones((8, wide.shape[1]), jnp.bfloat16)
    norms = lax.dot_general(ones, high, NT, preferred_element_type=jnp.float32)
    norms += lax.dot_general(ones, low, NT, preferred_element_type=jnp.float32)
    for message in (right, left):
        for k, part in enumerate(split(norms[0:1, :])):
            message[knn : knn + 1, k * block_rows : (k + 1) * block_rows] = part


def join_body(pad, right_block, left_block, right_lists, left_lists, right, left):
    rows = right_block.shape[0]
    for block, lists, out in ((right_block, right_lists, right), (left_block, left_lists, left)):
        out[0:pad, :] = lists[0:pad, :]
        out[pad : pad + rows, :] = block[...]
        kept = out.shape[0] - rows
        if kept > pad:
            out[pad + rows :, :] = lists[pad:kept, :]


def histogram(entry, knn, block_rows):
    width = 4 if knn < 16 else 8
    per = 32 // width
    shift = {4: 3, 8: 2}[width]
    value = entry.astype(jnp.float32).astype(jnp.int32)
    word = value >> shift
    bit = jnp.left_shift(jnp.int32(1), (value & (per - 1)) * width)
    words = block_rows // per
    index = lax.broadcasted_iota(jnp.int32, (words, block_rows), 0)
    total = jnp.zeros((words, block_rows), jnp.int32)
    for k in range(knn):
        total += jnp.where(word[k : k + 1, :] == index, bit[k : k + 1, :], 0)
    amount = (lax.broadcasted_iota(jnp.int32, (words, per, block_rows), 1)) * width
    spread = jnp.broadcast_to(total[:, None, :], (words, per, block_rows))
    counts = lax.shift_right_logical(spread, amount) & ((1 << width) - 1)
    return counts.reshape(block_rows, block_rows)


def own_counts_body(knn, own, out):
    block_rows = out.shape[1]
    for place in range(out.shape[0]):
        counts = histogram(own[place], knn, block_rows)
        out[place] = counts.astype(jnp.float32).astype(out.dtype)


def split(weight):
    high = weight.astype(jnp.bfloat16)
    return high, (weight - high.astype(jnp.float32)).astype(jnp.bfloat16)


NT = (((1,), (1,)), ((), ()))


def rows_of(refs, pieces):
    parts = [refs[k][a:b, :] for k, a, b in pieces]
    return parts[0] if len(parts) == 1 else jnp.concatenate(parts, axis=0)


def entry_of(refs, spot, pad, block_rows):
    k, row, column = spot
    return refs[k][row : row + pad, column : column + block_rows]


def identity_of(rows):
    row = lax.broadcasted_iota(jnp.int32, (rows, rows), 0)
    column = lax.broadcasted_iota(jnp.int32, (rows, rows), 1)
    return jnp.where(row == column, 1.0, 0.0).astype(jnp.bfloat16)


def transposed(counts):
    return lax.dot_general(identity_of(counts.shape[0]), counts, NT, preferred_element_type=jnp.float32)


def norm_parts(message, knn, block_rows):
    row = message[knn : knn + 1, :].astype(jnp.float32)
    return row[:, :block_rows], row[:, block_rows:]


def norm_table(parts, features, mine):
    high = float(features >> max(features.bit_length() - 8, 0) << max(features.bit_length() - 8, 0))
    fixed = (1.0, 1.0, high, features - high) if mine else (1.0, 1.0, 1.0, 1.0)
    own_first = 0 if mine else 2
    block_rows = parts[0].shape[1]
    row = lax.broadcasted_iota(jnp.int32, (16, block_rows), 0)
    table = jnp.zeros((16, block_rows), jnp.float32)
    for k, value in ((2 - own_first, fixed[0]), (3 - own_first, fixed[1]), (4, fixed[2]), (5, fixed[3])):
        table = jnp.where(row == k, value, table)
    for k, part in enumerate(parts):
        table = jnp.where(row == own_first + k, part, table)
    return table.astype(jnp.bfloat16)


TN = (((0,), (0,)), ((), ()))
CHUNK = 32


def fold(value):
    rows, lanes = value.shape
    return jnp.sum(value.reshape(rows // 8, 8, lanes), axis=0)


def kernel_phase(a, a_norms, b, b_norms, present, counts, constants, out, totals, weight=1.0):
    features = constants[0]
    base = lax.dot_general(
        norm_table(a_norms, features, True),
        norm_table(b_norms, features, False),
        TN,
        preferred_element_type=jnp.float32,
    )
    inner = lax.dot_general(a * -2.0, b, NT, preferred_element_type=jnp.float32)
    block_rows = a.shape[0]
    for start in range(0, block_rows, CHUNK):
        rows = slice(start, start + CHUNK)
        scaled = base[rows] + inner[rows]
        kernel = (present * (features * weight)) / scaled
        if out is not None:
            out[rows, :] = kernel
        if totals is not None:
            logs = jnp.log(scaled * (1.0 / features))
            totals[0] += fold(kernel)
            totals[1] += fold((weight * counts[rows]) * logs)


def pull_phase(remote, kernel, counts, weights, pulls_in, rows_in, pulls, row_sums):
    block_rows = remote.shape[0]
    for start in range(0, block_rows, CHUNK):
        rows = slice(start, start + CHUNK)
        value = kernel[rows, :]
        near = counts[rows, :].astype(jnp.float32) * value
        far = value * value
        for k, weight in enumerate((near, far)):
            total = jnp.sum(weight, axis=1, keepdims=True)
            if rows_in is not None:
                total += rows_in[k, rows, :]
            row_sums[k, rows, :] = total
        high, low = split(near)
        for k, part in enumerate((high, low, far.astype(jnp.bfloat16))):
            weights[k * block_rows + start : k * block_rows + start + CHUNK, :] = part
    product = jnp.dot(weights[...], remote, preferred_element_type=jnp.float32)
    near = product[:block_rows] + product[block_rows : 2 * block_rows]
    far = product[2 * block_rows :]
    pulls[0] = near if pulls_in is None else near + pulls_in[0]
    pulls[1] = far if pulls_in is None else far + pulls_in[1]


def tile_counts(own, entry, knn):
    back = histogram(entry, knn, own.shape[0]).astype(jnp.float32)
    present = jnp.where(entry[0:1, :].astype(jnp.float32) <= float(own.shape[0]), 1.0, 0.0)
    return transposed(own) + back, present


def step_body(tiles, counted, first, constants, *refs):
    _, knn, pad = constants
    local_ref, note_ref, own_ref = refs[:3]
    kernel, weights = refs[-2:]
    held_count = 3 if counted else 2
    held = refs[-2 - held_count : -2]
    held_in = [None] * 3 if first else refs[-2 - 2 * held_count : -2 - held_count]
    sources = refs[3 : len(refs) - 2 - held_count * (1 if first else 2)]
    local = local_ref[...]
    block_rows = local.shape[0]
    local_norms = norm_parts(note_ref, knn, block_rows)
    totals = None
    if counted:
        if first:
            zero = jnp.zeros((8, block_rows), jnp.float32)
            totals = [zero, zero]
        else:
            totals = [held_in[2][0], held_in[2][1]]
    for number, (place, pieces, front, spot) in enumerate(tiles):
        remote = rows_of(sources, pieces)
        entry = entry_of(sources, spot, pad, block_rows)
        counts, present = tile_counts(own_ref[place], entry, knn)
        remote_norms = norm_parts(sources[front], knn, block_rows)
        kernel_phase(local, local_norms, remote, remote_norms, present, counts, constants, kernel, totals)
        before = held if number else held_in
        pull_phase(remote, kernel, counts, weights, before[0], before[1], held[0], held[1])
    if counted:
        held[2][0] = totals[0]
        held[2][1] = totals[1]


def sums_body(tiles, pairs, constants, *refs):
    _, knn, pad = constants
    local_ref, note_ref, own_ref, base_ref, sums_in = refs[:5]
    row_ref, kernels, all_counts = refs[-3:]
    sources = refs[5:-3]
    local = local_ref[...]
    block_rows = local.shape[0]
    local_norms = norm_parts(note_ref, knn, block_rows)
    totals = [sums_in[0], sums_in[1]]
    for number, (place, pieces, front, spot) in enumerate(tiles):
        remote = rows_of(sources, pieces)
        entry = entry_of(sources, spot, pad, block_rows)
        counts, present = tile_counts(own_ref[place], entry, knn)
        all_counts[number] = counts.astype(all_counts.dtype)
        remote_norms = norm_parts(sources[front], knn, block_rows)
        kernel_phase(
            local, local_norms, remote, remote_norms, present, counts, constants, kernels.at[number], totals
        )
    for left_pieces, left_front, right_pieces, right_front, there, back, weight in pairs:
        entry = entry_of(sources, there, pad, block_rows)
        forward = histogram(entry, knn, block_rows).astype(jnp.float32).astype(jnp.bfloat16)
        counts, present = tile_counts(forward, entry_of(sources, back, pad, block_rows), knn)
        kernel_phase(
            rows_of(sources, left_pieces),
            norm_parts(sources[left_front], knn, block_rows),
            rows_of(sources, right_pieces),
            norm_parts(sources[right_front], knn, block_rows),
            present,
            counts,
            constants,
            None,
            totals,
            weight,
        )
    lane = lax.broadcasted_iota(jnp.int32, row_ref.shape, 1)
    row = jnp.where(lane == 0, jnp.sum(totals[0]), base_ref[...])
    row_ref[...] = jnp.where(lane == 1, jnp.sum(totals[1]) * -0.5, row)


def pull_body(tiles, *refs):
    kernels, counts = refs[:2]
    pulls_in, rows_in, pulls, row_sums, weights = refs[-5:]
    sources = refs[2:-5]
    for number, (_, pieces, _, _) in enumerate(tiles):
        before = (pulls, row_sums) if number else (pulls_in, rows_in)
        pull_phase(
            rows_of(sources, pieces), kernels.at[number], counts.at[number], weights, *before, pulls, row_sums
        )


def finish_body(groups, features, table, *refs):
    windows = refs[: len(table)]
    local_ref, pulls, row_sums, gradient, loss, relative = refs[len(table) :]
    for ref, rows in zip(windows, table):
        for row, offset in rows:
            relative[offset : offset + 1, :] = ref[row : row + 1, :]
    me = ring_position(lax.axis_index("wide"), groups)
    summed = jnp.sum(pltpu.roll(relative[...], me, 0), axis=0, keepdims=True)
    lane = lax.broadcasted_iota(jnp.int32, summed.shape, 1)

    def pick(k):
        return jnp.sum(jnp.where(lane == k, summed, 0.0), axis=1, keepdims=True)

    total, attract, edges, entries = pick(0), pick(1), pick(2), pick(3)
    loss[...] = -attract / edges + jnp.log(total / entries)
    repulsion = 2.0 * edges / total
    scale = 2.0 / features
    near_scale, far_scale = scale, scale * repulsion
    for start in range(0, gradient.shape[0], CHUNK):
        chunk = slice(start, start + CHUNK)
        rows = near_scale * row_sums[0, chunk, :] - far_scale * row_sums[1, chunk, :]
        pull = near_scale * pulls[0, chunk, :] - far_scale * pulls[1, chunk, :]
        gradient[chunk, :] = rows * local_ref[chunk, :].astype(jnp.float32) - pull


def column_step(embeddings, partners, pair_kind, neighbors):
    block_rows, features = embeddings.shape
    knn = neighbors.shape[1]
    pad = list_rows(knn)
    groups = lax.axis_size("wide")
    half, quarter = groups // 2, groups // 4
    offsets = ring_offsets(groups)
    places = len(offsets)
    place_of = {offset: place for place, offset in enumerate(offsets)}
    tails = tail_groups(groups)
    list_height = pad * (len(tails) + 1)
    lists = jax.ShapeDtypeStruct((list_height, features), embeddings.dtype)

    def send(value, offset):
        return lax.ppermute(value, "wide", shift_pairs(groups, offset))

    def both(right, left):
        return [send(right, 1), send(left, -1)]

    def height(step):
        return pad * (1 + sum(far >= step for _, far in tails))

    blocks = both(embeddings, embeddings)
    right_note, left_note, own, base, local = pl.pallas_call(
        functools.partial(prepare_body, groups, offsets),
        out_shape=[
            lists,
            lists,
            jax.ShapeDtypeStruct((places, pad, block_rows), jnp.bfloat16),
            jax.ShapeDtypeStruct((1, 128), jnp.float32),
            jax.ShapeDtypeStruct(embeddings.shape, embeddings.dtype),
        ],
        in_specs=[pl.BlockSpec(memory_space=pltpu.HBM)] * 4,
        out_specs=[VMEM] * 5,
        scratch_shapes=[
            pltpu.SMEM(partners.shape, jnp.int32),
            pltpu.SMEM(pair_kind.shape, jnp.int32),
            pltpu.VMEM(neighbors.shape, jnp.int32),
            pltpu.SemaphoreType.DMA((4,)),
        ],
        compiler_params=compiler_params(8),
        cost_estimate=cost(1.5),
        name="prepare",
    )(*(pltpu.with_memory_space_constraint(x, pltpu.HBM) for x in (partners, pair_kind, neighbors, embeddings)))
    notes = both(right_note, left_note)
    own_counts = pl.pallas_call(
        functools.partial(own_counts_body, knn),
        out_shape=jax.ShapeDtypeStruct((places, block_rows, block_rows), jnp.bfloat16),
        in_specs=[VMEM],
        out_specs=VMEM,
        compiler_params=compiler_params(8),
        cost_estimate=cost(1.0),
        name="own_counts",
    )(own)
    middle = block_rows // 2
    halves = [[block[:middle] for block in blocks], [block[middle:] for block in blocks]]
    arrived = {1: [blocks[0], blocks[1], *notes]}
    for step in range(2, quarter + 1):
        plain = both(*halves[0])
        other = both(*halves[1])
        halves = [plain, other]
        notes = [
            send(note[: height(step)], sign * step)
            for note, sign in ((right_note, 1), (left_note, -1))
        ]
        arrived[step] = plain + other + notes
    message = jax.ShapeDtypeStruct((middle + height(quarter + 1), features), embeddings.dtype)
    noted = pl.pallas_call(
        functools.partial(join_body, pad),
        out_shape=[message, message],
        in_specs=[VMEM] * 4,
        out_specs=[VMEM] * 2,
        compiler_params=compiler_params(4),
        cost_estimate=cost(0.3),
        name="join",
    )(*halves[1], *notes)
    plain = halves[0]
    for step in range(quarter + 1, half):
        plain = both(*plain)
        noted = both(*(note[: middle + height(step)] for note in noted))
        arrived[step] = plain + noted
    arrived[half] = [send(plain[1], -1), send(noted[0][: middle + pad], 1)]

    def front_of(step, side):
        if step == half:
            return 1
        return side + 4 if 1 < step <= quarter else side + 2

    def spot_of(step, side, distance):
        row, column = list_spot(groups, distance, block_rows, pad)
        return front_of(step, side), row + (middle if row and step > quarter else 0), column

    def block_of(step, side):
        if step == 1:
            return [(side, 0, block_rows)]
        if step <= quarter:
            return [(side, 0, middle), (side + 2, 0, middle)]
        if step == half:
            return [(0, 0, middle), (1, pad, pad + middle)]
        return [(side, 0, middle), (side + 2, pad, pad + middle)]

    def tiles_of(step):
        if step == half:
            return [(place_of[half], block_of(step, 0), front_of(step, 0), spot_of(step, 0, half))]
        return [
            (place_of[sign * step], block_of(step, side), front_of(step, side), spot_of(step, side, step))
            for side, sign in ((0, -1), (1, 1))
        ]

    def call(body, operands, shapes, time, aliases=None, scratch=()):
        return pl.pallas_call(
            body,
            out_shape=shapes,
            in_specs=[VMEM] * len(operands),
            out_specs=[VMEM] * len(shapes),
            scratch_shapes=list(scratch),
            input_output_aliases=aliases or {},
            compiler_params=compiler_params(12),
            cost_estimate=cost(time),
        )(*operands)

    constants = (features, knn, pad)
    square = (block_rows, block_rows)
    scratch = [
        pltpu.VMEM(square, jnp.float32),
        pltpu.VMEM((3 * block_rows, block_rows), jnp.bfloat16),
    ]
    held = [
        jax.ShapeDtypeStruct((2, block_rows, features), jnp.float32),
        jax.ShapeDtypeStruct((2, block_rows, 1), jnp.float32),
        jax.ShapeDtypeStruct((2, 8, block_rows), jnp.float32),
    ]
    common = [local, right_note, own_counts]
    state = None
    for step in range(1, half + 1):
        tiles = tiles_of(step)
        if step == quarter:
            sources, pairs = list(arrived[step]), []
            for distance in range(quarter + 1, half + 1):
                lower = distance - quarter
                base_at, factor = 0, 1.0
                if lower != quarter:
                    base_at, factor = len(sources), 2.0
                    sources += arrived[lower]
                pairs.append(
                    (
                        [(at + base_at, low, high) for at, low, high in block_of(lower, 0)],
                        front_of(lower, 0) + base_at,
                        block_of(step, 1),
                        front_of(step, 1),
                        (front_of(lower, 0) + base_at, *spot_of(lower, 0, distance)[1:]),
                        spot_of(step, 1, distance),
                        factor,
                    )
                )
            window, kernels, counts = call(
                functools.partial(sums_body, tiles, pairs, constants),
                common + [base, state[2]] + sources,
                [
                    jax.ShapeDtypeStruct((1, 128), jnp.float32),
                    jax.ShapeDtypeStruct((2, *square), jnp.float32),
                    jax.ShapeDtypeStruct((2, *square), jnp.bfloat16),
                ],
                1.8,
            )
            operands = [kernels, counts] + arrived[step]
            state = call(
                functools.partial(pull_body, tiles),
                operands + list(state[:2]),
                held[:2],
                1.5,
                {len(operands) + k: k for k in range(2)},
                scratch[1:],
            )
            continue
        counted = step < quarter
        operands = common + arrived[step]
        shapes = held if counted else held[:2]
        first = state is None
        aliases = {} if first else {len(operands) + k: k for k in range(len(shapes))}
        state = call(
            functools.partial(step_body, tiles, counted, first, constants),
            operands + ([] if first else list(state)),
            shapes,
            2.0,
            aliases,
            scratch,
        )
    columns = lax.axis_size("narrow")
    bit = 1
    while bit < columns:
        other = lax.ppermute(window, "narrow", [(k, k ^ bit) for k in range(columns)])
        window = window + other
        bit *= 2
    reach, received = 0, []
    table = [[(0, 0)]]
    while 2 * reach + 1 < groups:
        if reach:
            window = jnp.concatenate([received[1], window, received[0]], axis=0)
            table = [[(row, (row - reach) % groups) for row in range(2 * reach + 1)]]
        stride = 2 * reach + 1
        received = [send(window, -stride), send(window, stride)]
        seen = {offset for _, offset in table[0]}
        for sign in (1, -1):
            rows = []
            for row in range(2 * reach + 1):
                offset = (sign * stride + row - reach) % groups
                if offset not in seen:
                    seen.add(offset)
                    rows.append((row, offset))
            table.append(rows)
        reach = 3 * reach + 1
    gradient, loss = call(
        functools.partial(finish_body, groups, features, table),
        [window, *received, local, *state],
        [
            jax.ShapeDtypeStruct((block_rows, features), jnp.float32),
            jax.ShapeDtypeStruct((1, 1), jnp.float32),
        ],
        1.0,
        None,
        [pltpu.VMEM((groups, 128), jnp.float32)],
    )
    return gradient, loss.reshape(())


def solution(mesh):
    in_specs = (P(AXES, None), P(AXES, None), P(AXES, None), P(None, None, AXES))
    return jax.shard_map(
        column_step, mesh=mesh, in_specs=in_specs, out_specs=(P(AXES, None), P()), check_vma=False
    )
```

```python
import functools

import jax
import jax.numpy as jnp
from jax import lax
from jax.experimental import pallas as pl
from jax.experimental.pallas import tpu as pltpu
from jax.sharding import PartitionSpec as P


AXES = ("wide", "narrow")
VMEM = pl.BlockSpec(memory_space=pltpu.VMEM)
SMEM = pl.BlockSpec(memory_space=pltpu.SMEM)


def ring_position(index, groups):
    return jnp.where(index % 2 == 0, index // 2, groups - 1 - index // 2)


def ring_index(position, groups):
    return jnp.where(position < groups // 2, 2 * position, 2 * (groups - position) - 1)


def ring_order(groups):
    half = groups // 2
    return [2 * q if q < half else 2 * (groups - q) - 1 for q in range(groups)]


def shift_pairs(groups, offset):
    order = ring_order(groups)
    return [(order[q], order[(q + offset) % groups]) for q in range(groups)]


def ring_offsets(groups):
    half = groups // 2
    offsets = []
    for step in range(1, half):
        offsets += [step, -step]
    return offsets + [half]


def list_rows(knn):
    return (knn // 16 + 1) * 16


def tail_groups(groups):
    half = groups // 2
    return [(a, a + 1) for a in range(half - 3, 0, -2)]


def list_spot(groups, distance, block_rows, pad):
    half = groups // 2
    if distance >= half - 1:
        return 0, (distance - half + 1) * block_rows
    for group, (near, far) in enumerate(tail_groups(groups)):
        if distance in (near, far):
            return pad * (group + 1), (distance - near) * block_rows
    raise ValueError


def compiler_params(mib):
    return pltpu.CompilerParams(vmem_limit_bytes=mib << 20)


def cost(microseconds):
    return pl.CostEstimate(
        flops=int(microseconds * 8e8), bytes_accessed=int(microseconds * 2e6), transcendentals=0
    )


def prepare_body(groups, offsets, *refs):
    inputs, (right, left, own, base, local) = refs[:4], refs[4:9]
    partners, marks, neighbors, sems = refs[9:]
    copies = [
        pltpu.make_async_copy(source, held, sems.at[k])
        for k, (source, held) in enumerate(zip(inputs, (partners, marks, neighbors, local)))
    ]
    for copy in copies:
        copy.start()
    for copy in copies[:3]:
        copy.wait()
    knn, block_rows = neighbors.shape[1:]
    pad = own.shape[1]
    half = groups // 2
    me = ring_position(lax.axis_index("wide"), groups)
    slots = partners.shape[1]
    marked_total = jnp.int32(0)
    present_total = jnp.int32(0)
    for place, offset in enumerate(offsets):
        target = ring_index(lax.rem(me + offset + groups, groups), groups)
        slot = jnp.int32(0)
        present = jnp.int32(0)
        marked = jnp.int32(0)
        for s in range(slots):
            hit = (partners[0, s] == target).astype(jnp.int32)
            slot += hit * s
            present += hit
            marked += hit * marks[0, s]
        marked_total += marked
        present_total += present
        empty = jnp.where(present > 0, block_rows, 2 * block_rows)
        rows = jnp.where(marked > 0, neighbors[slot], empty).astype(jnp.float32)
        filler = jnp.zeros((pad - knn, block_rows), jnp.float32)
        entry = jnp.concatenate([rows, filler], axis=0).astype(jnp.bfloat16)
        own[place] = entry
        row, column = list_spot(groups, abs(offset), block_rows, pad)
        for message in (right, left) if offset == half else (right,) if offset > 0 else (left,):
            message[row : row + pad, column : column + block_rows] = entry
    lane = lax.broadcasted_iota(jnp.int32, base.shape, 1)
    edges = marked_total.astype(jnp.float32) * float(knn * block_rows)
    entries = present_total.astype(jnp.float32) * float(block_rows * block_rows)
    base[...] = jnp.where(lane == 2, edges, jnp.where(lane == 3, entries, 0.0))
    copies[3].wait()
    wide = local[...].astype(jnp.float32)
    high, low = split(wide * wide)
    ones = jnp.ones((8, wide.shape[1]), jnp.bfloat16)
    norms = lax.dot_general(ones, high, NT, preferred_element_type=jnp.float32)
    norms += lax.dot_general(ones, low, NT, preferred_element_type=jnp.float32)
    for message in (right, left):
        for k, part in enumerate(split(norms[0:1, :])):
            message[knn : knn + 1, k * block_rows : (k + 1) * block_rows] = part


def join_body(pad, right_block, left_block, right_lists, left_lists, right, left):
    rows = right_block.shape[0]
    for block, lists, out in ((right_block, right_lists, right), (left_block, left_lists, left)):
        out[0:pad, :] = lists[0:pad, :]
        out[pad : pad + rows, :] = block[...]
        kept = out.shape[0] - rows
        if kept > pad:
            out[pad + rows :, :] = lists[pad:kept, :]


def histogram(entry, knn, block_rows):
    width = 4 if knn < 16 else 8
    per = 32 // width
    shift = {4: 3, 8: 2}[width]
    value = entry.astype(jnp.float32).astype(jnp.int32)
    word = value >> shift
    bit = jnp.left_shift(jnp.int32(1), (value & (per - 1)) * width)
    words = block_rows // per
    index = lax.broadcasted_iota(jnp.int32, (words, block_rows), 0)
    total = jnp.zeros((words, block_rows), jnp.int32)
    for k in range(knn):
        total += jnp.where(word[k : k + 1, :] == index, bit[k : k + 1, :], 0)
    amount = (lax.broadcasted_iota(jnp.int32, (words, per, block_rows), 1)) * width
    spread = jnp.broadcast_to(total[:, None, :], (words, per, block_rows))
    counts = lax.shift_right_logical(spread, amount) & ((1 << width) - 1)
    return counts.reshape(block_rows, block_rows)


def split(weight):
    high = weight.astype(jnp.bfloat16)
    return high, (weight - high.astype(jnp.float32)).astype(jnp.bfloat16)


NT = (((1,), (1,)), ((), ()))


def rows_of(refs, pieces):
    parts = [refs[k][a:b, :] for k, a, b in pieces]
    return parts[0] if len(parts) == 1 else jnp.concatenate(parts, axis=0)


def entry_of(refs, spot, pad, block_rows):
    k, row, column = spot
    return refs[k][row : row + pad, column : column + block_rows]


def identity_of(rows):
    row = lax.broadcasted_iota(jnp.int32, (rows, rows), 0)
    column = lax.broadcasted_iota(jnp.int32, (rows, rows), 1)
    return jnp.where(row == column, 1.0, 0.0).astype(jnp.bfloat16)


def transposed(counts):
    return lax.dot_general(identity_of(counts.shape[0]), counts, NT, preferred_element_type=jnp.float32)


def norm_parts(message, knn, block_rows):
    row = message[knn : knn + 1, :].astype(jnp.float32)
    return row[:, :block_rows], row[:, block_rows:]


def norm_table(parts, features, mine):
    high = float(features >> max(features.bit_length() - 8, 0) << max(features.bit_length() - 8, 0))
    fixed = (1.0, 1.0, high, features - high) if mine else (1.0, 1.0, 1.0, 1.0)
    own_first = 0 if mine else 2
    block_rows = parts[0].shape[1]
    row = lax.broadcasted_iota(jnp.int32, (16, block_rows), 0)
    table = jnp.zeros((16, block_rows), jnp.float32)
    for k, value in ((2 - own_first, fixed[0]), (3 - own_first, fixed[1]), (4, fixed[2]), (5, fixed[3])):
        table = jnp.where(row == k, value, table)
    for k, part in enumerate(parts):
        table = jnp.where(row == own_first + k, part, table)
    return table.astype(jnp.bfloat16)


TN = (((0,), (0,)), ((), ()))
CHUNK = 32


def fold(value):
    rows, lanes = value.shape
    return jnp.sum(value.reshape(rows // 8, 8, lanes), axis=0)


def kernel_phase(a, a_norms, b, b_norms, present, counts, constants, out, totals, weight=1.0):
    features = constants[0]
    base = lax.dot_general(
        norm_table(a_norms, features, True),
        norm_table(b_norms, features, False),
        TN,
        preferred_element_type=jnp.float32,
    )
    inner = lax.dot_general(a * -2.0, b, NT, preferred_element_type=jnp.float32)
    block_rows = a.shape[0]
    for start in range(0, block_rows, CHUNK):
        rows = slice(start, start + CHUNK)
        scaled = base[rows] + inner[rows]
        kernel = (present * (features * weight)) / scaled
        if out is not None:
            out[rows, :] = kernel
        if totals is not None:
            logs = jnp.log(scaled * (1.0 / features))
            totals[0] += fold(kernel)
            totals[1] += fold((weight * counts[rows]) * logs)


def pull_phase(remote, kernel, counts, weights, pulls_in, rows_in, pulls, row_sums):
    block_rows = remote.shape[0]
    for start in range(0, block_rows, CHUNK):
        rows = slice(start, start + CHUNK)
        value = kernel[rows, :]
        near = counts[rows, :].astype(jnp.float32) * value
        far = value * value
        for k, weight in enumerate((near, far)):
            total = jnp.sum(weight, axis=1, keepdims=True)
            if rows_in is not None:
                total += rows_in[k, rows, :]
            row_sums[k, rows, :] = total
        high, low = split(near)
        for k, part in enumerate((high, low, far.astype(jnp.bfloat16))):
            weights[k * block_rows + start : k * block_rows + start + CHUNK, :] = part
    product = jnp.dot(weights[...], remote, preferred_element_type=jnp.float32)
    near = product[:block_rows] + product[block_rows : 2 * block_rows]
    far = product[2 * block_rows :]
    pulls[0] = near if pulls_in is None else near + pulls_in[0]
    pulls[1] = far if pulls_in is None else far + pulls_in[1]


def present_row(entry):
    return jnp.where(entry[0:1, :].astype(jnp.float32) <= float(entry.shape[1]), 1.0, 0.0)


def tile_counts(own, entry, knn):
    back = histogram(entry, knn, own.shape[0]).astype(jnp.float32)
    return transposed(own) + back, present_row(entry)


def forward_counts(entry, knn):
    return histogram(entry, knn, entry.shape[1]).astype(jnp.float32).astype(jnp.bfloat16)


def counts_body(tiles, pairs, knn, pad, *refs):
    own, *notes, near, rest = refs
    block_rows = near.shape[1]
    for number, (place, spot) in enumerate(tiles):
        entry = entry_of(notes, spot, pad, block_rows)
        counts, _ = tile_counts(forward_counts(own[place], knn), entry, knn)
        near[number] = counts.astype(near.dtype)
    for number, (there, back) in enumerate(pairs):
        forward = forward_counts(entry_of(notes, there, pad, block_rows), knn)
        counts, _ = tile_counts(forward, entry_of(notes, back, pad, block_rows), knn)
        near[len(tiles) + number] = counts.astype(near.dtype)
    for number in range(rest.shape[0]):
        rest[number] = forward_counts(own[len(tiles) + number], knn)


def step_body(tiles, near, skipped, counted, first, constants, *refs):
    _, knn, pad = constants
    local_ref, note_ref, own_ref = refs[:3]
    kernel, weights = refs[-2:]
    held_count = 3 if counted else 2
    held = refs[-2 - held_count : -2]
    held_in = [None] * 3 if first else refs[-2 - 2 * held_count : -2 - held_count]
    sources = refs[3 : len(refs) - 2 - held_count * (1 if first else 2)]
    local = local_ref[...]
    block_rows = local.shape[0]
    local_norms = norm_parts(note_ref, knn, block_rows)
    totals = None
    if counted:
        if first:
            zero = jnp.zeros((8, block_rows), jnp.float32)
            totals = [zero, zero]
        else:
            totals = [held_in[2][0], held_in[2][1]]
    for number, (place, pieces, front, spot) in enumerate(tiles):
        remote = rows_of(sources, pieces)
        entry = entry_of(sources, spot, pad, block_rows)
        if near is None:
            counts, present = tile_counts(own_ref[place - skipped], entry, knn)
        else:
            counts, present = own_ref[near + number].astype(jnp.float32), present_row(entry)
        remote_norms = norm_parts(sources[front], knn, block_rows)
        kernel_phase(local, local_norms, remote, remote_norms, present, counts, constants, kernel, totals)
        before = held if number else held_in
        pull_phase(remote, kernel, counts, weights, before[0], before[1], held[0], held[1])
    if counted:
        held[2][0] = totals[0]
        held[2][1] = totals[1]


def sums_body(tiles, pairs, near, near_pairs, constants, *refs):
    _, knn, pad = constants
    local_ref, note_ref, own_ref, base_ref, sums_in = refs[:5]
    row_ref, kernels = refs[-2:]
    sources = refs[5:-2]
    local = local_ref[...]
    block_rows = local.shape[0]
    local_norms = norm_parts(note_ref, knn, block_rows)
    totals = [sums_in[0], sums_in[1]]
    for number, (place, pieces, front, spot) in enumerate(tiles):
        remote = rows_of(sources, pieces)
        entry = entry_of(sources, spot, pad, block_rows)
        counts, present = own_ref[near + number].astype(jnp.float32), present_row(entry)
        remote_norms = norm_parts(sources[front], knn, block_rows)
        kernel_phase(
            local, local_norms, remote, remote_norms, present, counts, constants, kernels.at[number], totals
        )
    for number, (left_pieces, left_front, right_pieces, right_front, _, back, weight) in enumerate(pairs):
        counts = own_ref[near_pairs + number].astype(jnp.float32)
        present = present_row(entry_of(sources, back, pad, block_rows))
        kernel_phase(
            rows_of(sources, left_pieces),
            norm_parts(sources[left_front], knn, block_rows),
            rows_of(sources, right_pieces),
            norm_parts(sources[right_front], knn, block_rows),
            present,
            counts,
            constants,
            None,
            totals,
            weight,
        )
    lane = lax.broadcasted_iota(jnp.int32, row_ref.shape, 1)
    row = jnp.where(lane == 0, jnp.sum(totals[0]), base_ref[...])
    row_ref[...] = jnp.where(lane == 1, jnp.sum(totals[1]) * -0.5, row)


def pull_body(tiles, near, *refs):
    kernels, counts = refs[:2]
    pulls_in, rows_in, pulls, row_sums, weights = refs[-5:]
    sources = refs[2:-5]
    for number, (_, pieces, _, _) in enumerate(tiles):
        before = (pulls, row_sums) if number else (pulls_in, rows_in)
        pull_phase(
            rows_of(sources, pieces), kernels.at[number], counts.at[near + number], weights, *before, pulls, row_sums
        )


def finish_body(groups, features, table, *refs):
    windows = refs[: len(table)]
    local_ref, pulls, row_sums, gradient, loss, relative = refs[len(table) :]
    for ref, rows in zip(windows, table):
        for row, offset in rows:
            relative[offset : offset + 1, :] = ref[row : row + 1, :]
    me = ring_position(lax.axis_index("wide"), groups)
    summed = jnp.sum(pltpu.roll(relative[...], me, 0), axis=0, keepdims=True)
    lane = lax.broadcasted_iota(jnp.int32, summed.shape, 1)

    def pick(k):
        return jnp.sum(jnp.where(lane == k, summed, 0.0), axis=1, keepdims=True)

    total, attract, edges, entries = pick(0), pick(1), pick(2), pick(3)
    loss[...] = -attract / edges + jnp.log(total / entries)
    repulsion = 2.0 * edges / total
    scale = 2.0 / features
    near_scale, far_scale = scale, scale * repulsion
    for start in range(0, gradient.shape[0], CHUNK):
        chunk = slice(start, start + CHUNK)
        rows = near_scale * row_sums[0, chunk, :] - far_scale * row_sums[1, chunk, :]
        pull = near_scale * pulls[0, chunk, :] - far_scale * pulls[1, chunk, :]
        gradient[chunk, :] = rows * local_ref[chunk, :].astype(jnp.float32) - pull


def column_step(embeddings, partners, pair_kind, neighbors):
    block_rows, features = embeddings.shape
    knn = neighbors.shape[1]
    pad = list_rows(knn)
    groups = lax.axis_size("wide")
    half, quarter = groups // 2, groups // 4
    offsets = ring_offsets(groups)
    places = len(offsets)
    place_of = {offset: place for place, offset in enumerate(offsets)}
    tails = tail_groups(groups)
    list_height = pad * (len(tails) + 1)
    lists = jax.ShapeDtypeStruct((list_height, features), embeddings.dtype)

    def send(value, offset):
        return lax.ppermute(value, "wide", shift_pairs(groups, offset))

    def both(right, left):
        return [send(right, 1), send(left, -1)]

    def height(step):
        return pad * (1 + sum(far >= step for _, far in tails))

    blocks = both(embeddings, embeddings)
    right_note, left_note, own, base, local = pl.pallas_call(
        functools.partial(prepare_body, groups, offsets),
        out_shape=[
            lists,
            lists,
            jax.ShapeDtypeStruct((places, pad, block_rows), jnp.bfloat16),
            jax.ShapeDtypeStruct((1, 128), jnp.float32),
            jax.ShapeDtypeStruct(embeddings.shape, embeddings.dtype),
        ],
        in_specs=[pl.BlockSpec(memory_space=pltpu.HBM)] * 4,
        out_specs=[VMEM] * 5,
        scratch_shapes=[
            pltpu.SMEM(partners.shape, jnp.int32),
            pltpu.SMEM(pair_kind.shape, jnp.int32),
            pltpu.VMEM(neighbors.shape, jnp.int32),
            pltpu.SemaphoreType.DMA((4,)),
        ],
        compiler_params=compiler_params(8),
        cost_estimate=cost(1.5),
        name="prepare",
    )(*(pltpu.with_memory_space_constraint(x, pltpu.HBM) for x in (partners, pair_kind, neighbors, embeddings)))
    notes = both(right_note, left_note)
    middle = block_rows // 2
    halves = [[block[:middle] for block in blocks], [block[middle:] for block in blocks]]
    arrived = {1: [blocks[0], blocks[1], *notes]}
    for step in range(2, quarter + 1):
        plain = both(*halves[0])
        other = both(*halves[1])
        halves = [plain, other]
        notes = [send(note[: height(step)], sign * step) for note, sign in ((right_note, 1), (left_note, -1))]
        arrived[step] = plain + other + notes
    message = jax.ShapeDtypeStruct((middle + height(quarter + 1), features), embeddings.dtype)
    noted = pl.pallas_call(
        functools.partial(join_body, pad),
        out_shape=[message, message],
        in_specs=[VMEM] * 4,
        out_specs=[VMEM] * 2,
        compiler_params=compiler_params(4),
        cost_estimate=cost(0.3),
        name="join",
    )(*halves[1], *notes)
    plain = halves[0]
    for step in range(quarter + 1, half):
        plain = both(*plain)
        noted = both(*(note[: middle + height(step)] for note in noted))
        arrived[step] = plain + noted
    arrived[half] = [send(plain[1], -1), send(noted[0][: middle + pad], 1)]

    def front_of(step, side):
        if step == half:
            return 1
        return side + 4 if 1 < step <= quarter else side + 2

    def spot_of(step, side, distance):
        row, column = list_spot(groups, distance, block_rows, pad)
        return front_of(step, side), row + (middle if row and step > quarter else 0), column

    def block_of(step, side):
        if step == 1:
            return [(side, 0, block_rows)]
        if step <= quarter:
            return [(side, 0, middle), (side + 2, 0, middle)]
        if step == half:
            return [(0, 0, middle), (1, pad, pad + middle)]
        return [(side, 0, middle), (side + 2, pad, pad + middle)]

    def tiles_of(step):
        if step == half:
            return [(place_of[half], block_of(step, 0), front_of(step, 0), spot_of(step, 0, half))]
        return [
            (place_of[sign * step], block_of(step, side), front_of(step, side), spot_of(step, side, step))
            for side, sign in ((0, -1), (1, 1))
        ]

    def call(body, operands, shapes, time, aliases=None, scratch=()):
        return pl.pallas_call(
            body,
            out_shape=shapes,
            in_specs=[VMEM] * len(operands),
            out_specs=[VMEM] * len(shapes),
            scratch_shapes=list(scratch),
            input_output_aliases=aliases or {},
            compiler_params=compiler_params(12),
            cost_estimate=cost(time),
        )(*operands)

    constants = (features, knn, pad)
    square = (block_rows, block_rows)
    scratch = [
        pltpu.VMEM(square, jnp.float32),
        pltpu.VMEM((3 * block_rows, block_rows), jnp.bfloat16),
    ]
    held = [
        jax.ShapeDtypeStruct((2, block_rows, features), jnp.float32),
        jax.ShapeDtypeStruct((2, block_rows, 1), jnp.float32),
        jax.ShapeDtypeStruct((2, 8, block_rows), jnp.float32),
    ]
    near_tiles, near_pairs = [], []
    for step in range(1, quarter + 1):
        for side, sign in ((0, -1), (1, 1)):
            _, row, column = spot_of(step, side, step)
            near_tiles.append((place_of[sign * step], (2 * step - 2 + side, row, column)))
    for distance in range(quarter + 1, half + 1):
        lower = distance - quarter
        there = (2 * lower - 2, *spot_of(lower, 0, distance)[1:])
        near_pairs.append((there, (2 * quarter - 1, *spot_of(quarter, 1, distance)[1:])))
    near_counts, own_counts = call(
        functools.partial(counts_body, near_tiles, near_pairs, knn, pad),
        [own] + [note for step in range(1, quarter + 1) for note in arrived[step][-2:]],
        [
            jax.ShapeDtypeStruct((len(near_tiles) + len(near_pairs), *square), jnp.bfloat16),
            jax.ShapeDtypeStruct((places - len(near_tiles), *square), jnp.bfloat16),
        ],
        1.6,
    )
    common = [local, right_note, own_counts]
    nearby = [local, right_note, near_counts]
    state = None
    for step in range(1, half + 1):
        tiles = tiles_of(step)
        if step == quarter:
            sources, pairs = list(arrived[step]), []
            for distance in range(quarter + 1, half + 1):
                lower = distance - quarter
                base_at, factor = 0, 1.0
                if lower != quarter:
                    base_at, factor = len(sources), 2.0
                    sources += arrived[lower]
                pairs.append(
                    (
                        [(at + base_at, low, high) for at, low, high in block_of(lower, 0)],
                        front_of(lower, 0) + base_at,
                        block_of(step, 1),
                        front_of(step, 1),
                        (front_of(lower, 0) + base_at, *spot_of(lower, 0, distance)[1:]),
                        spot_of(step, 1, distance),
                        factor,
                    )
                )
            window, kernels = call(
                functools.partial(sums_body, tiles, pairs, 2 * step - 2, len(near_tiles), constants),
                nearby + [base, state[2]] + sources,
                [
                    jax.ShapeDtypeStruct((1, 128), jnp.float32),
                    jax.ShapeDtypeStruct((2, *square), jnp.float32),
                ],
                1.2,
            )
            operands = [kernels, near_counts] + arrived[step]
            state = call(
                functools.partial(pull_body, tiles, 2 * step - 2),
                operands + list(state[:2]),
                held[:2],
                1.5,
                {len(operands) + k: k for k in range(2)},
                scratch[1:],
            )
            continue
        counted = step < quarter
        operands = (nearby if counted else common) + arrived[step]
        shapes = held if counted else held[:2]
        first = state is None
        aliases = {} if first else {len(operands) + k: k for k in range(len(shapes))}
        state = call(
            functools.partial(
                step_body, tiles, 2 * step - 2 if counted else None, 2 * quarter, counted, first, constants
            ),
            operands + ([] if first else list(state)),
            shapes,
            2.0,
            aliases,
            scratch,
        )
    columns = lax.axis_size("narrow")
    bit = 1
    while bit < columns:
        other = lax.ppermute(window, "narrow", [(k, k ^ bit) for k in range(columns)])
        window = window + other
        bit *= 2
    reach, received = 0, []
    table = [[(0, 0)]]
    while 2 * reach + 1 < groups:
        if reach:
            window = jnp.concatenate([received[1], window, received[0]], axis=0)
            table = [[(row, (row - reach) % groups) for row in range(2 * reach + 1)]]
        stride = 2 * reach + 1
        received = [send(window, -stride), send(window, stride)]
        seen = {offset for _, offset in table[0]}
        for sign in (1, -1):
            rows = []
            for row in range(2 * reach + 1):
                offset = (sign * stride + row - reach) % groups
                if offset not in seen:
                    seen.add(offset)
                    rows.append((row, offset))
            table.append(rows)
        reach = 3 * reach + 1
    gradient, loss = call(
        functools.partial(finish_body, groups, features, table),
        [window, *received, local, *state],
        [
            jax.ShapeDtypeStruct((block_rows, features), jnp.float32),
            jax.ShapeDtypeStruct((1, 1), jnp.float32),
        ],
        1.0,
        None,
        [pltpu.VMEM((groups, 128), jnp.float32)],
    )
    return gradient, loss.reshape(())


def solution(mesh):
    in_specs = (P(AXES, None), P(AXES, None), P(AXES, None), P(None, None, AXES))
    return jax.shard_map(column_step, mesh=mesh, in_specs=in_specs, out_specs=(P(AXES, None), P()), check_vma=False)
```
